32 devices in a mesh: rows: 8 (over y, x, core), blk: 4 (over z).
Axes of the slice: x: 2, y: 2, z: 4, core: 2. Of those that a mesh axis runs over, the one named last changes fastest.
Arguments:
- vectors: float32 [6144, 128], P('blk'), may hold values from -6 to 6
- left_intersection: float32 [256, 128, 128], P(('rows', 'blk')), may hold values from -0.5 to 0.5
- right_intersection: float32 [48, 128, 128], P('blk'), may hold values from -0.5 to 0.5
- tiles: float32 [512, 128, 128], P('rows'), may hold values from -0.09375 to 0.09375
- pair_cols: int32 [256, 32], P(('rows', 'blk')), may hold values from 0 to 47, all different within a row
- pair_owner: int32 [256, 32], P(('rows', 'blk')), may hold values from 0 to 7, as said below
- pair_slot: int32 [256, 32], P(('rows', 'blk')), may hold values from 0 to 63
- pair_counts: int32 [256], P(('rows', 'blk')), may hold values from 1 to 32, as said below
Outputs:
- product: float32 [32768, 128], P(('rows', 'blk'))
The draws below stay inside these ranges and needn't reach their ends.
Inputs may be any that keep to these rules, and one draw needn't show every extreme that they name: `pair_owner`: among the 256 entries of each aligned block of 8 row blocks, every rows index appears exactly 32 times. `pair_cols`: the column blocks listed for one row block are distinct. `pair_counts`: some row block has all 32 entries live.
All inputs are finite; a program needn't handle non-finite values.
Results may differ from the reference program's by a relative error of at most 0.0003.
Values sent between devices are 32-bit elements; how exact they have to be, the bound alone decides.
No kernel may reach another device: no remote copies, remote signals or barrier semaphores. Data moves between devices by JAX's collectives and lax.ppermute only.
A program may use at most 128 MiB of HBM per device.

```python
import math
import jax
import jax.numpy as jnp
import numpy as np
from jax import lax

FB = 128
TILE = 128
VECS = 128
CAP = 32
TILES_DEV = 64
RB_DEV = 8
ROW_BLOCKS = 256
ROWS = 32768
COLS = 6144
COL_BLOCKS = 48
TILES = 512
N_ROWS = 8


def draw_pair_owner(key, part):
    device_count = ROW_BLOCKS // RB_DEV
    subkeys = jax.random.split(jax.random.fold_in(key, 11), device_count)

    def draw_device(subkey):
        return jax.random.permutation(subkey, RB_DEV * CAP) % N_ROWS
    owners = jax.vmap(draw_device)(subkeys)
    return owners.reshape(ROW_BLOCKS, CAP).astype(jnp.int32)


def draw_pair_counts(key, part):
    first, second, third = jax.random.split(jax.random.fold_in(key, 23), 3)
    device_count = ROW_BLOCKS // RB_DEV
    shifts = jax.random.randint(first, (device_count,), 0, 2)
    device_top = jnp.maximum(jnp.right_shift(jnp.full((device_count,), CAP, jnp.int32), shifts), 1)
    tops = jnp.repeat(device_top, RB_DEV)
    halves = tops // 2
    raw_draw = jax.random.randint(second, (ROW_BLOCKS,), 0, 1 << 20)
    counts = halves + raw_draw % (tops - halves) + 1
    full_row = jax.random.randint(third, (), 0, ROW_BLOCKS)
    counts = jnp.where(jnp.arange(ROW_BLOCKS) == full_row, CAP, counts)
    return counts.astype(jnp.int32)


def place_ends(result, rng, smallest, largest):
    shape = result.shape
    place = [jax.random.randint(jax.random.fold_in(rng, axis), (), 0, shape[axis]) for axis in range(len(shape))]
    result = result.at[tuple(place)].set(smallest)
    longest = shape.index(max(shape))
    place[longest] = (place[longest] + 1) % shape[longest]
    return result.at[tuple(place)].set(largest)


def block_scale(rng, dims, cuts, least, high):
    level, own = 1.0, jax.random.fold_in(rng, 6)
    for axis_at, blocks in cuts:
        steps = jnp.exp(jax.random.uniform(jax.random.fold_in(own, axis_at), (blocks,), jnp.float32, least / len(cuts), high / len(cuts)))
        level = level * jnp.repeat(steps, dims[axis_at] // blocks).reshape([-1 if axis == axis_at else 1 for axis in range(len(dims))])
    return level


def rank_table(number_of, slope):
    portions = [(1 << 20) // math.isqrt(standing ** slope) + 1 for standing in range(1, number_of + 1)]
    width = 1 + sum(portions) // (1 << 30)
    return np.cumsum(np.array([max(1, weight // width) for weight in portions]))


def ranked(stream_key, dims, count, lean):
    table = rank_table(count, lean)
    ticket = jax.random.randint(jax.random.fold_in(stream_key, 1), dims, 0, int(table[count - 1]))
    standing = jnp.searchsorted(jnp.asarray(table, jnp.int32), ticket, side="right")
    return jax.random.permutation(jax.random.fold_in(stream_key, 2), count)[standing].astype(jnp.int32)


def distinct(key, rows, count, top, lift):
    sequence = jax.random.permutation(jax.random.fold_in(key, 1), count)
    boost = sequence
    for power in range(3):
        boost = boost * boost // count
    boost = boost * lift // count
    tickets = jax.random.randint(jax.random.fold_in(key, 2), (rows, count), 0, 4096) + boost
    holders = jax.random.permutation(jax.random.fold_in(key, 3), rows)[jnp.arange(count) % rows]
    tickets = jnp.where(jnp.arange(rows)[:, None] == holders[None, :], 1 << 14, tickets)
    score = tickets * count + jnp.arange(count)
    return lax.top_k(score.astype(jnp.int32), top)[1].astype(jnp.int32)


def bell_draw(own_key, dims, width, reach, cuts=(), dtype=jnp.bfloat16):
    gain = block_scale(own_key, dims, cuts, -0.22, 0.18) if cuts else 1.0
    result = jax.random.normal(own_key, dims, jnp.float32) * width * gain
    return jnp.minimum(jnp.maximum(result, -reach), reach).astype(dtype)


def setup_inputs(seed: int = 0) -> dict:
    streams_of = jax.random.split(jax.random.key(seed), 9)
    return {
        "vectors": bell_draw(streams_of[0], (COLS, VECS), 1.0, 6.0, ((0, 4),), jnp.float32),
        "left_intersection": bell_draw(streams_of[1], (ROW_BLOCKS, FB, TILE), TILE ** -0.5, 0.5, ((0, 32),), jnp.float32),
        "right_intersection": bell_draw(streams_of[2], (COL_BLOCKS, FB, TILE), FB ** -0.5, 0.5, ((0, 4),), jnp.float32),
        "tiles": bell_draw(streams_of[3], (TILES, TILE, TILE), (TILE * CAP) ** -0.5, 0.09375, ((0, 8),), jnp.float32),
        "pair_cols": distinct(streams_of[4], ROW_BLOCKS, COL_BLOCKS, CAP, 0),
        "pair_owner": draw_pair_owner(jax.random.fold_in(streams_of[8], 71), 0),
        "pair_slot": place_ends(ranked(streams_of[6], (ROW_BLOCKS, CAP), TILES_DEV, 2), jax.random.fold_in(streams_of[6], 3), 0, TILES_DEV - 1).astype(jnp.int32),
        "pair_counts": draw_pair_counts(jax.random.fold_in(streams_of[8], 71), 0),
    }


def row_block(left_block, col_ids, tile_ids, count, tiles, projected):
    live_mask = (jnp.arange(CAP) < count).astype(jnp.float32)
    chosen = jnp.take(tiles, tile_ids, axis=0) * live_mask[:, None, None]
    picked = jnp.take(projected, col_ids, axis=0)
    summed = jnp.einsum("gtu,guv->tv", chosen, picked, precision=lax.Precision.HIGHEST)
    return jnp.dot(left_block, summed, precision=lax.Precision.HIGHEST, preferred_element_type=jnp.float32)


def reference(vectors, left_intersection, right_intersection, tiles, pair_cols, pair_owner, pair_slot, pair_counts):
    blocked = vectors.reshape(COL_BLOCKS, FB, VECS)
    projected = jnp.einsum("csu,csv->cuv", right_intersection, blocked, precision=lax.Precision.HIGHEST)
    tile_ids = (pair_owner * TILES_DEV + pair_slot).astype(jnp.int32)

    def per_block(packed):
        left_block, col_ids, ids_here, count = packed
        return row_block(left_block, col_ids, ids_here, count, tiles, projected)

    blocks_out = lax.map(per_block, (left_intersection, pair_cols, tile_ids, pair_counts))
    return blocks_out.reshape(ROWS, VECS)
```

```python
import functools

import jax
import jax.numpy as jnp
from jax import lax
from jax.experimental import pallas as pl
from jax.experimental.pallas import tpu as pltpu
from jax.sharding import PartitionSpec as P

F32 = jnp.float32
BF16 = jnp.bfloat16
I32 = jnp.int32
HIGHEST = lax.Precision.HIGHEST
GROUP = 2
UNROLL = 8
MIB = 1 << 20


VMEM = pl.BlockSpec(memory_space=pltpu.VMEM)
SMEM = pl.BlockSpec(memory_space=pltpu.SMEM)


def cost(flops, nbytes):
    return pl.CostEstimate(flops=flops, bytes_accessed=nbytes, transcendentals=0)


def split(x):
    hi = x.astype(BF16)
    return hi, (x - hi.astype(F32)).astype(BF16)


def project(v, r):
    return lax.dot_general(
        v, r, (((0,), (0,)), ((), ())), precision=HIGHEST, preferred_element_type=F32
    )


def send_kernel(place, v_ref, r_ref, out_ref, full):
    groups, count, width, _ = out_ref.shape
    quarter, part = place[0], place[1]
    for i in range(count):
        full[...] = project(v_ref[quarter * count + i], r_ref[quarter * count + i])
        for g in range(groups):
            p = lax.rem(part + g, groups)
            out_ref[g, i] = full[pl.ds(pl.multiple_of(p * width, width), width), :]


def own_kernel(place, v_ref, r_ref, out_ref, full):
    count, width, _ = out_ref.shape
    part = place[1]
    start = pl.multiple_of(part * width, width)

    def one(i, _):
        full[...] = project(v_ref[i], r_ref[i])
        out_ref[i] = full[pl.ds(start, width), :]
        return 0

    lax.fori_loop(0, count, one, 0)


def list_kernel(held, cols, owner, slot, counts, out_ref, fill):
    chips, _, cap = out_ref.shape
    blocks, listed = cols.shape
    for c in range(chips):
        fill[c] = 0

    def row(i, _):
        def entry(e, _):
            o = owner[i, e]
            c = o // 2
            n = fill[c]
            out_ref[c, 0, n] = (o % 2) * held + slot[i, e]
            out_ref[c, 1, n] = cols[i, e]
            out_ref[c, 2, n] = i
            fill[c] = n + 1
            return 0

        lax.fori_loop(0, counts[i], entry, 0)
        return 0

    lax.fori_loop(0, blocks, row, 0)
    for c in range(chips):
        n = fill[c]
        out_ref[c, 3, 0] = n

        def pad(j, _):
            out_ref[c, 0, j] = 0
            out_ref[c, 1, j] = 0
            out_ref[c, 2, j] = blocks
            return 0

        lax.fori_loop(n, jnp.minimum(n + UNROLL, cap), pad, 0)


def tile_kernel(core, own_ref, other_ref, out_ref):
    count, _, width = own_ref.shape
    mine = (pl.program_id(0) == core[0])

    def run(src):
        for i in range(count):
            hi, lo = split(src[i].T)
            out_ref[i, :, :width] = hi
            out_ref[i, :, width:] = lo

    @pl.when(mine)
    def _():
        run(own_ref)

    @pl.when(jnp.logical_not(mine))
    def _():
        run(other_ref)


def gather_kernel(planes, place, own_ref, *refs):
    pieces, out_ref = refs[:-1], refs[-1]
    count, width, _ = own_ref.shape
    quarter = count // 4
    blk = place[2]

    def put(src, start, n):
        for i in range(n):
            hi, lo = split(src[i])
            out_ref[start + i, :width] = hi
            out_ref[start + i, width:] = lo

    put(own_ref, blk * count, count)
    for k in range(1, planes):
        plane = lax.rem(blk - k + planes, planes)
        for p in range(4):
            put(pieces[(k - 1) * 4 + p], plane * count + place[3 + p] * quarter, quarter)


def entry_kernel(lists, tiles_ref, proj_ref, out_ref, acc):
    blocks, width, coarse = out_ref.shape
    acc[...] = jnp.zeros_like(acc)

    def step(s, _):
        base = s * UNROLL
        terms = []
        for u in range(UNROLL):
            d = jnp.dot(
                proj_ref[lists[1, base + u]],
                tiles_ref[lists[0, base + u]],
                preferred_element_type=F32,
            )
            terms.append(d[:width, :coarse] + d[width:, :coarse] + d[:width, coarse:])
        for u in range(UNROLL):
            acc[lists[2, base + u]] += terms[u]
        return 0

    lax.fori_loop(0, (lists[3, 0] + UNROLL - 1) // UNROLL, step, 0)
    out_ref[...] = acc[:blocks]


def final_kernel(place, left_ref, own_a, own_b, own_c, *refs):
    others, out_ref, summed = refs[:-2], refs[-2], refs[-1]
    blocks, width, _ = own_a.shape
    groups = len(others) + 1
    part = place[1]
    for i in range(blocks):
        for g in range(groups):
            p = lax.rem(part + g, groups)
            val = own_a[i] + own_b[i] + own_c[i] if g == 0 else others[g - 1][i]
            summed[pl.ds(pl.multiple_of(p * width, width), width), :] = val
        out_ref[i] = lax.dot_general(
            left_ref[i], summed[...], (((1,), (1,)), ((), ())),
            precision=HIGHEST, preferred_element_type=F32,
        )


def call(kernel, prefetch, ins, out, scratch, args, name, estimate, limit, grid=(), out_spec=VMEM):
    return pl.pallas_call(
        kernel,
        out_shape=out,
        grid_spec=pltpu.PrefetchScalarGridSpec(
            num_scalar_prefetch=prefetch,
            grid=grid,
            in_specs=ins,
            out_specs=out_spec,
            scratch_shapes=scratch,
        ),
        compiler_params=pltpu.CompilerParams(vmem_limit_bytes=limit),
        cost_estimate=estimate,
        name=name,
    )(*args)


def per_device(
    vectors, left, right, tiles, pair_cols, pair_owner, pair_slot, pair_counts
):
    rows, planes = lax.axis_size("rows"), lax.axis_size("blk")
    row, blk = lax.axis_index("rows"), lax.axis_index("blk")
    blocks, fine, coarse = left.shape
    vecs = vectors.shape[1]
    count = right.shape[0]
    held = tiles.shape[0]
    listed = pair_cols.shape[1]
    chips = rows // 2
    bits = chips.bit_length() - 1
    cap = blocks * listed // chips
    width = vecs // GROUP
    quarter = count // 4
    core, chip = row % 2, row // 2
    b0, b1 = chip % 2, (chip // 2) % 2
    part = blk % GROUP

    def physical(mask, core_at):
        return mask if core_at == 0 else (mask & ~3) | ((mask & 1) << 1) | ((mask >> 1) & 1)

    def across(mask):
        return [(r, r ^ (physical(mask, r % 2) << 1)) for r in range(rows)]

    def swap(x):
        return lax.ppermute(x, "rows", [(r, r ^ 1) for r in range(rows)])

    def turn(x, k):
        return lax.ppermute(x, "blk", [(b, (b + k) % planes) for b in range(planes)])

    def mates(x, g):
        return lax.ppermute(
            x, "blk", [(b, b // GROUP * GROUP + (b + g) % GROUP) for b in range(planes)]
        )

    mine = jnp.where(core == 0, b0, 2 + b1)
    theirs = jnp.where(core == 0, 2 + b1, b0)
    place = jnp.stack([mine, part, blk, mine, mine ^ 1, theirs, theirs ^ 1]).astype(I32)

    v = vectors.reshape(count, fine, vecs)
    sent = call(
        send_kernel, 1, [VMEM, VMEM],
        jax.ShapeDtypeStruct((GROUP, quarter, width, coarse), F32),
        [pltpu.VMEM((vecs, coarse), F32)],
        (place, v, right), "send", cost(2 * quarter * 128**3 * 6, 2 * count * 65536), 8 * MIB,
    )
    arrived = {k: turn(sent[k % GROUP], k) for k in range(1, planes)}
    other_tiles = swap(tiles)

    lists = call(
        functools.partial(list_kernel, held), 0, [SMEM] * 4,
        jax.ShapeDtypeStruct((chips, 4, cap), I32),
        [pltpu.SMEM((chips,), I32)],
        (pair_cols, pair_owner, pair_slot, pair_counts), "lists", cost(10000, 4096), 4 * MIB,
        out_spec=SMEM,
    )
    gathered = jnp.stack([lists] + [mates(lists, g) for g in range(1, GROUP)], axis=1)
    tables = {}
    for m in range(chips):
        to_chip = chip ^ jnp.where(core == 0, physical(m, 0), physical(m, 1))
        chosen = lax.dynamic_index_in_dim(gathered, to_chip, 0, keepdims=False)
        tables[m] = chosen if m == 0 else lax.ppermute(chosen, "rows", across(m))

    own = call(
        own_kernel, 1, [VMEM, VMEM],
        jax.ShapeDtypeStruct((count, width, coarse), F32),
        [pltpu.VMEM((vecs, coarse), F32)],
        (place, v, right), "own", cost(2 * count * 128**3 * 6, 2 * count * 65536), 8 * MIB,
    )
    step = 8
    nstep = held // step
    packed = call(
        tile_kernel, 1,
        [
            pl.BlockSpec((step, coarse, coarse), lambda c, i, core: (jnp.where(c == core[0], i, nstep - 1), 0, 0)),
            pl.BlockSpec((step, coarse, coarse), lambda c, i, core: (jnp.where(c == core[0], 0, i), 0, 0)),
        ],
        jax.ShapeDtypeStruct((2 * held, coarse, 2 * coarse), BF16),
        [], (core.reshape(1).astype(I32), tiles, other_tiles), "tiles",
        cost(held * 65536 * 4, held * 65536 * 4), 8 * MIB, grid=(2, nstep),
        out_spec=pl.BlockSpec((step, coarse, 2 * coarse), lambda c, i, core: (c * nstep + i, 0, 0)),
    )

    pieces = []
    for k in range(1, planes):
        z = arrived[k]
        x = lax.ppermute(z, "rows", across(1))
        pieces += [z, x, swap(z), swap(x)]
    proj = call(
        functools.partial(gather_kernel, planes), 1, [VMEM] * (1 + len(pieces)),
        jax.ShapeDtypeStruct((planes * count, 2 * width, coarse), BF16),
        [], (place, own, *pieces), "gather", cost(10**6, 2 * planes * count * 32768), 16 * MIB,
    )

    def partial_sum(m, g):
        return call(
            entry_kernel, 1, [VMEM, VMEM],
            jax.ShapeDtypeStruct((blocks, width, coarse), F32),
            [pltpu.VMEM((blocks + 1, width, coarse), F32)],
            (tables[m][g], packed, proj), f"entries{m}_{g}",
            cost(cap * 128**3 * 8, 4 * MIB), 24 * MIB,
        )

    def reduce_over_chips(g):
        total = {m: [partial_sum(m, g)] for m in range(chips)}
        for j in range(bits):
            bit = 1 << j
            for m in sorted((m for m in range(chips) if m & bit and not m & (bit - 1)), reverse=True):
                value = functools.reduce(jnp.add, total[m])
                total[m ^ bit].append(lax.ppermute(value, "rows", across(bit)))
        return total[0]

    others = []
    for g in range(1, GROUP):
        value = functools.reduce(jnp.add, reduce_over_chips(g))
        others.append(mates(value, GROUP - g))
    mine_sum = reduce_over_chips(0)
    while len(mine_sum) > 3:
        mine_sum = [mine_sum[0] + mine_sum[1]] + mine_sum[2:]
    result = call(
        final_kernel, 1, [VMEM] * (4 + len(others)),
        jax.ShapeDtypeStruct((blocks, fine, vecs), F32),
        [pltpu.VMEM((vecs, coarse), F32)],
        (place, left, *mine_sum, *others), "final", cost(2 * blocks * 128**3 * 6, 2 * MIB), 8 * MIB,
    )
    return result.reshape(blocks * fine, vecs)


def solution(mesh):
    return jax.shard_map(
        per_device,
        mesh=mesh,
        in_specs=(
            P("blk", None),
            P(("rows", "blk"), None, None),
            P("blk", None, None),
            P("rows", None, None),
            P(("rows", "blk"), None),
            P(("rows", "blk"), None),
            P(("rows", "blk"), None),
            P(("rows", "blk")),
        ),
        out_specs=P(("rows", "blk"), None),
        check_vma=False,
    )
```

```python
import functools

import jax
import jax.numpy as jnp
from jax import lax
from jax.experimental import pallas as pl
from jax.experimental.pallas import tpu as pltpu
from jax.sharding import PartitionSpec as P


F32 = jnp.float32
BF16 = jnp.bfloat16
I32 = jnp.int32
UNROLL = 8
MIB = 1 << 20


VMEM = pl.BlockSpec(memory_space=pltpu.VMEM)
HBM = pl.BlockSpec(memory_space=pltpu.HBM)
SMEM = pl.BlockSpec(memory_space=pltpu.SMEM)


def in_hbm(x):
    return pltpu.with_memory_space_constraint(x, pltpu.HBM)


def cost(flops, nbytes):
    return pl.CostEstimate(flops=flops, bytes_accessed=nbytes, transcendentals=0)


def split(x):
    hi = x.astype(BF16)
    return hi, (x - hi.astype(F32)).astype(BF16)


def lanes(shape):
    return lax.broadcasted_iota(I32, shape, len(shape) - 1)


def triple(a, b, dims):
    a_hi, a_lo = split(a)
    b_hi, b_lo = split(b)

    def dot(x, y):
        return lax.dot_general(x, y, (dims, ((), ())), preferred_element_type=F32)

    return dot(a_hi, b_hi) + dot(a_hi, b_lo) + dot(a_lo, b_hi)


def fold_halves(x):
    half = x.shape[0] // 2
    top, bottom = x[:half], x[half:]
    low = lanes(top.shape) < half
    first = jnp.where(low, top, pltpu.roll(bottom, half, 1))
    second = jnp.where(low, pltpu.roll(top, half, 1), bottom)
    return first, second


def unfold_halves(first, second):
    half = first.shape[0]
    low = lanes(first.shape) < half
    top = jnp.where(low, first, pltpu.roll(second, half, 1))
    bottom = jnp.where(low, pltpu.roll(first, half, 1), second)
    return top, bottom


def send_kernel(place, v_ref, r_ref, out_ref, v_buf, r_buf, sems):
    part = place[1]
    count = v_buf.shape[0]
    first_block = place[0] * count
    copies = [
        pltpu.make_async_copy(ref.at[pl.ds(first_block, count)], buf, sems.at[i])
        for i, (ref, buf) in enumerate(((v_ref, v_buf), (r_ref, r_buf)))
    ]
    for copy in copies:
        copy.start()
    for copy in copies:
        copy.wait()
    for i in range(count):
        first, second = fold_halves(triple(r_buf[i], v_buf[i], ((0,), (0,))))
        out_ref[part, i] = first
        out_ref[1 - part, i] = second


def own_kernel(place, v_ref, r_ref, out_ref, v_buf, r_buf, sems):
    keep_first = place[1] == 0
    count = v_buf.shape[0]
    copies = [
        pltpu.make_async_copy(ref, buf, sems.at[i])
        for i, (ref, buf) in enumerate(((v_ref, v_buf), (r_ref, r_buf)))
    ]
    for copy in copies:
        copy.start()
    for copy in copies:
        copy.wait()
    for i in range(count):
        first, second = fold_halves(triple(r_buf[i], v_buf[i], ((0,), (0,))))
        out_ref[i] = jnp.where(keep_first, first, second)


def list_kernel(chips, held, cols, owner, slot, counts, out_ref, words, sems):
    blocks, listed = cols.shape
    span = out_ref.shape[2]
    copies = [
        pltpu.make_async_copy(ref, words.at[i], sems.at[i])
        for i, ref in enumerate((cols, owner, slot))
    ]
    for copy in copies:
        copy.start()
    for copy in copies:
        copy.wait()
    kinds = lax.broadcasted_iota(I32, (16, listed), 0)
    upto = lax.broadcasted_iota(I32, (listed, listed), 0) <= lanes((listed, listed))
    upto = upto.astype(F32).astype(BF16)
    spots = lax.broadcasted_iota(I32, (chips * span, listed), 0).astype(F32)
    offset = jnp.zeros((16, 1), F32)
    total = jnp.zeros((8, chips * span), F32)
    for i in range(blocks):
        col, own, place = words[0, i : i + 1], words[1, i : i + 1], words[2, i : i + 1]
        chip = jnp.where(lanes((1, listed)) < counts[i], own >> 1, chips)
        match = (kinds == chip).astype(F32)
        ranks = jnp.dot(match.astype(BF16), upto, preferred_element_type=F32) + offset
        offset = offset + jnp.sum(match, axis=1, keepdims=True)
        rank = jnp.sum(match * ranks, axis=0, keepdims=True) - 1
        target = jnp.where(chip < chips, chip.astype(F32) * span + rank, -1.0)
        chosen = (spots == target).astype(F32).astype(BF16)
        one = jnp.ones((1, listed), F32)
        fields = jnp.concatenate(
            [
                one,
                ((own & 1) * held + place).astype(F32),
                col.astype(F32),
                one * (i - blocks),
                jnp.zeros((4, listed), F32),
            ],
            axis=0,
        )
        total += lax.dot_general(
            fields.astype(BF16), chosen, (((1,), (1,)), ((), ())), preferred_element_type=F32
        )
    row = lax.broadcasted_iota(I32, (8, span), 0)
    for c in range(chips):
        part = total[:, c * span : (c + 1) * span]
        number = jnp.broadcast_to(offset[c : c + 1], (8, span))
        part = jnp.where(row == 0, number, jnp.where(row == 3, part + blocks, part))
        out_ref[c] = part[:4].astype(I32)


def tile_kernel(core, own_ref, other_ref, out_ref, buf, sems):
    held, _, width = own_ref.shape
    step = buf.shape[1]
    steps = held // step
    mine = core[0]
    refs = (own_ref, other_ref)

    def copy(s):
        ref, at = refs[s // steps], s % steps * step
        return pltpu.make_async_copy(ref.at[pl.ds(at, step)], buf.at[s % 2], sems.at[s % 2])

    copy(0).start()
    for s in range(2 * steps):
        if s + 1 < 2 * steps:
            copy(s + 1).start()
        copy(s).wait()
        whose = mine if s < steps else 1 - mine
        start = whose * held + s % steps * step

        def one(i, _):
            hi, lo = split(buf[s % 2, i])
            out_ref[start + i, :, :width] = hi
            out_ref[start + i, :, width:] = lo
            return 0

        lax.fori_loop(0, step, one, 0, unroll=4)


def gather_kernel(planes, place, own_ref, *refs):
    pieces, out_ref = refs[:-1], refs[-1]
    count, half, width = own_ref.shape
    quarter = count // 4
    blk = place[2]
    low = lanes((half, width)) < half
    zero = jnp.zeros((half, width), F32)

    def put(src, start, n):
        for i in range(n):
            x = src[i]
            hi = x.astype(BF16).astype(F32)
            lo = pltpu.roll(x - hi, half, 1)
            out_ref[start + i, 0 * half : 1 * half] = jnp.where(low, hi, lo).astype(BF16)
            out_ref[start + i, 1 * half : 2 * half] = jnp.where(low, lo, hi).astype(BF16)
            out_ref[start + i, 2 * half : 3 * half] = jnp.where(low, hi, zero).astype(BF16)
            out_ref[start + i, 3 * half : 4 * half] = jnp.where(low, zero, hi).astype(BF16)

    put(own_ref, blk * count, count)
    for k in range(1, planes):
        plane = lax.rem(blk - k + planes, planes)
        for p in range(4):
            put(pieces[(k - 1) * 4 + p], plane * count + place[3 + p] * quarter, quarter)


def entry_kernel(g, lists, tiles_ref, proj_ref, out_ref, acc):
    blocks, half, width = out_ref.shape
    acc[...] = jnp.zeros_like(acc)

    def step(s, _):
        base = s * UNROLL
        terms = [
            jnp.dot(
                tiles_ref[lists[g, 1, base + u]],
                proj_ref[lists[g, 2, base + u]],
                preferred_element_type=F32,
            )
            for u in range(UNROLL)
        ]
        for u in range(UNROLL):
            acc[lists[g, 3, base + u]] += terms[u]
        return 0

    lax.fori_loop(0, (lists[g, 0, 0] + UNROLL - 1) // UNROLL, step, 0)
    low = lanes((half, width)) < half
    for i in range(blocks):
        top, bottom = acc[i, :half], acc[i, half:]
        a, b = jnp.where(low, top, bottom), jnp.where(low, bottom, top)
        out_ref[i] = a + pltpu.roll(b, half, 1)


def final_kernel(place, left_ref, own_a, own_b, own_c, other, out_ref):
    blocks, _, _ = own_a.shape
    keep_first = place[1] == 0
    for i in range(blocks):
        own = own_a[i] + own_b[i] + own_c[i]
        first = jnp.where(keep_first, own, other[i])
        second = jnp.where(keep_first, other[i], own)
        top, bottom = unfold_halves(first, second)
        summed = jnp.concatenate([top, bottom], axis=0)
        out_ref[i] = triple(left_ref[i], summed, ((1,), (0,)))


def call(kernel, prefetch, ins, out, scratch, args, estimate, limit, grid=(), out_spec=VMEM):
    return pl.pallas_call(
        kernel,
        out_shape=out,
        grid_spec=pltpu.PrefetchScalarGridSpec(
            num_scalar_prefetch=prefetch,
            grid=grid,
            in_specs=ins,
            out_specs=out_spec,
            scratch_shapes=scratch,
        ),
        compiler_params=pltpu.CompilerParams(vmem_limit_bytes=limit),
        cost_estimate=estimate,
    )(*args)


def work(
    vectors, left, right, tiles, pair_cols, pair_owner, pair_slot, pair_counts
):
    rows, planes = lax.axis_size("rows"), lax.axis_size("blk")
    row, blk = lax.axis_index("rows"), lax.axis_index("blk")
    blocks, fine, coarse = left.shape
    vecs = vectors.shape[1]
    count = right.shape[0]
    held = tiles.shape[0]
    listed = pair_cols.shape[1]
    chips = rows // 2
    bits = chips.bit_length() - 1
    cap = blocks * listed // chips
    half = coarse // 2
    quarter = count // 4
    core, chip = row & 1, row >> 1
    b0, b1 = chip & 1, (chip >> 1) & 1
    part = blk & 1

    def physical(mask, core_at):
        return mask if core_at == 0 else (mask & ~3) | ((mask & 1) << 1) | ((mask >> 1) & 1)

    def across(mask):
        return [(r, r ^ (physical(mask, r % 2) << 1)) for r in range(rows)]

    def swap(x):
        return lax.ppermute(x, "rows", [(r, r ^ 1) for r in range(rows)])

    def turn(x, k):
        return lax.ppermute(x, "blk", [(b, (b + k) % planes) for b in range(planes)])

    def mate(x):
        return lax.ppermute(x, "blk", [(b, b ^ 1) for b in range(planes)])

    mine = jnp.where(core == 0, b0, 2 + b1)
    theirs = jnp.where(core == 0, 2 + b1, b0)
    place = jnp.stack([mine, part, blk, mine, mine ^ 1, theirs, theirs ^ 1]).astype(I32)

    v = vectors.reshape(count, fine, vecs)
    v, right = in_hbm(v), in_hbm(right)

    def blocks_of(n):
        return [pltpu.VMEM((n, fine, vecs), F32)] * 2 + [pltpu.SemaphoreType.DMA((2,))]

    sent = call(
        send_kernel, 1, [HBM, HBM],
        jax.ShapeDtypeStruct((2, quarter, half, vecs), F32),
        blocks_of(quarter), (place, v, right),
        cost(2 * quarter * 128**3 * 3, 2 * quarter * 65536), 8 * MIB,
    )
    arrived = {k: turn(sent[k % 2], k) for k in range(1, planes)}
    other_tiles = swap(tiles)

    span = pl.cdiv(cap, 128) * 128
    lists = call(
        functools.partial(list_kernel, chips, held), 0, [HBM] * 3 + [SMEM],
        jax.ShapeDtypeStruct((chips, 4, span), I32),
        [pltpu.VMEM((3, blocks, listed), I32), pltpu.SemaphoreType.DMA((3,))],
        (in_hbm(pair_cols), in_hbm(pair_owner), in_hbm(pair_slot), pair_counts),
        cost(10**8, 16384), 8 * MIB,
    )
    gathered = jnp.stack([lists, mate(lists)], axis=1)
    tables = {}
    for m in range(chips):
        to_chip = chip ^ jnp.where(core == 0, physical(m, 0), physical(m, 1))
        chosen = lax.dynamic_index_in_dim(gathered, to_chip, 0, keepdims=False)
        tables[m] = chosen if m == 0 else lax.ppermute(chosen, "rows", across(m))

    own = call(
        own_kernel, 1, [HBM, HBM],
        jax.ShapeDtypeStruct((count, half, vecs), F32),
        blocks_of(count), (place, v, right), cost(2 * count * 128**3 * 3, 2 * count * 65536), 8 * MIB,
    )
    packed = call(
        tile_kernel, 1, [HBM, HBM],
        jax.ShapeDtypeStruct((2 * held, coarse, 2 * coarse), BF16),
        [pltpu.VMEM((2, 16, coarse, coarse), F32), pltpu.SemaphoreType.DMA((2,))],
        (core.reshape(1).astype(I32), in_hbm(tiles), in_hbm(other_tiles)),
        cost(held * 65536 * 4, held * 65536 * 4), 12 * MIB,
    )

    pieces = []
    for k in range(1, planes):
        z = arrived[k]
        x = lax.ppermute(z, "rows", across(1))
        pieces += [z, x, swap(z), swap(x)]
    proj = call(
        functools.partial(gather_kernel, planes), 1, [VMEM] * (1 + len(pieces)),
        jax.ShapeDtypeStruct((planes * count, 2 * coarse, vecs), BF16),
        [], (place, own, *pieces), cost(10**6, 3 * planes * count * 32768), 16 * MIB,
    )

    def partial_sum(m, g):
        return call(
            functools.partial(entry_kernel, g), 1, [VMEM, VMEM],
            jax.ShapeDtypeStruct((blocks, half, vecs), F32),
            [pltpu.VMEM((blocks + 1, coarse, vecs), F32)],
            (tables[m], packed, proj),
            cost(cap * 128**3 * 4, 4 * MIB), 12 * MIB,
        )

    def reduce_over_chips(g):
        total = {m: [partial_sum(m, g)] for m in range(chips)}
        for j in range(bits):
            bit = 1 << j
            for m in sorted((m for m in range(chips) if m & bit and not m & (bit - 1)), reverse=True):
                value = functools.reduce(jnp.add, total[m])
                total[m ^ bit].append(lax.ppermute(value, "rows", across(bit)))
        return total[0]

    other = mate(functools.reduce(jnp.add, reduce_over_chips(1)))
    sums = reduce_over_chips(0)
    while len(sums) > 3:
        sums = [sums[0] + sums[1]] + sums[2:]
    result = call(
        final_kernel, 1, [VMEM] * 5,
        jax.ShapeDtypeStruct((blocks, fine, vecs), F32),
        [], (place, left, *sums, other), cost(2 * blocks * 128**3 * 3, 2 * MIB), 8 * MIB,
    )
    return result.reshape(blocks * fine, vecs)


def solution(mesh):
    return jax.shard_map(
        work,
        mesh=mesh,
        in_specs=(
            P("blk", None),
            P(("rows", "blk"), None, None),
            P("blk", None, None),
            P("rows", None, None),
            P(("rows", "blk"), None),
            P(("rows", "blk"), None),
            P(("rows", "blk"), None),
            P(("rows", "blk")),
        ),
        out_specs=P(("rows", "blk"), None),
        check_vma=False,
    )
```

```python
import functools

import jax
import jax.numpy as jnp
from jax import lax
from jax.experimental import pallas as pl
from jax.experimental.pallas import tpu as pltpu
from jax.sharding import PartitionSpec as P


F32 = jnp.float32
BF16 = jnp.bfloat16
I32 = jnp.int32
UNROLL = 16
MIB = 1 << 20


VMEM = pl.BlockSpec(memory_space=pltpu.VMEM)
HBM = pl.BlockSpec(memory_space=pltpu.HBM)


def in_hbm(x):
    return pltpu.with_memory_space_constraint(x, pltpu.HBM)


def cost(flops, nbytes):
    return pl.CostEstimate(flops=flops, bytes_accessed=nbytes, transcendentals=0)


def split(x):
    hi = x.astype(BF16)
    return hi, (x - hi.astype(F32)).astype(BF16)


def lanes(shape):
    return lax.broadcasted_iota(I32, shape, len(shape) - 1)


def triple(a, b, dims):
    a_hi, a_lo = split(a)
    b_hi, b_lo = split(b)

    def dot(x, y):
        return lax.dot_general(x, y, (dims, ((), ())), preferred_element_type=F32)

    return dot(a_hi, b_hi) + dot(a_hi, b_lo) + dot(a_lo, b_hi)


def fold_halves(x):
    half = x.shape[0] // 2
    top, bottom = x[:half], x[half:]
    low = lanes(top.shape) < half
    first = jnp.where(low, top, pltpu.roll(bottom, half, 1))
    second = jnp.where(low, pltpu.roll(top, half, 1), bottom)
    return first, second


def unfold_halves(first, second):
    half = first.shape[0]
    low = lanes(first.shape) < half
    top = jnp.where(low, first, pltpu.roll(second, half, 1))
    bottom = jnp.where(low, pltpu.roll(first, half, 1), second)
    return top, bottom


def send_kernel(place, v_ref, r_ref, out_ref, v_buf, r_buf, sems):
    part = place[1]
    count = v_buf.shape[0]
    first_block = place[0] * count
    copies = [
        pltpu.make_async_copy(ref.at[pl.ds(first_block, count)], buf, sems.at[i])
        for i, (ref, buf) in enumerate(((v_ref, v_buf), (r_ref, r_buf)))
    ]
    for copy in copies:
        copy.start()
    for copy in copies:
        copy.wait()
    for i in range(count):
        first, second = fold_halves(triple(r_buf[i], v_buf[i], ((0,), (0,))))
        out_ref[part, i] = first
        out_ref[1 - part, i] = second


def own_kernel(place, v_ref, r_ref, out_ref, v_buf, r_buf, sems):
    keep_first = place[1] == 0
    count = v_buf.shape[0]
    copies = [
        pltpu.make_async_copy(ref, buf, sems.at[i])
        for i, (ref, buf) in enumerate(((v_ref, v_buf), (r_ref, r_buf)))
    ]
    for copy in copies:
        copy.start()
    for copy in copies:
        copy.wait()
    for i in range(count):
        first, second = fold_halves(triple(r_buf[i], v_buf[i], ((0,), (0,))))
        out_ref[i] = jnp.where(keep_first, first, second)


def list_kernel(chips, held, cols, owner, slot, number, out_ref, words, counts, sems):
    blocks, listed = cols.shape
    span = out_ref.shape[2]
    copies = [
        pltpu.make_async_copy(ref, words.at[i], sems.at[i])
        for i, ref in enumerate((cols, owner, slot))
    ]
    copies += [pltpu.make_async_copy(number, counts, sems.at[3])]
    for copy in copies:
        copy.start()
    for copy in copies:
        copy.wait()
    kinds = lax.broadcasted_iota(I32, (16, listed), 0)
    upto = lax.broadcasted_iota(I32, (listed, listed), 0) <= lanes((listed, listed))
    upto = upto.astype(F32).astype(BF16)
    spots = lax.broadcasted_iota(I32, (chips * span, listed), 0).astype(F32)
    offset = jnp.zeros((16, 1), F32)
    total = jnp.zeros((8, chips * span), F32)
    for i in range(blocks):
        col, own, place = words[0, i : i + 1], words[1, i : i + 1], words[2, i : i + 1]
        chip = jnp.where(lanes((1, listed)) < counts[i], own >> 1, chips)
        match = (kinds == chip).astype(F32)
        ranks = jnp.dot(match.astype(BF16), upto, preferred_element_type=F32) + offset
        offset = offset + jnp.sum(match, axis=1, keepdims=True)
        rank = jnp.sum(match * ranks, axis=0, keepdims=True) - 1
        target = jnp.where(chip < chips, chip.astype(F32) * span + rank, -1.0)
        chosen = (spots == target).astype(F32).astype(BF16)
        one = jnp.ones((1, listed), F32)
        fields = jnp.concatenate(
            [
                one,
                ((own & 1) * held + place).astype(F32),
                col.astype(F32),
                one * (i - blocks),
                jnp.zeros((4, listed), F32),
            ],
            axis=0,
        )
        total += lax.dot_general(
            fields.astype(BF16), chosen, (((1,), (1,)), ((), ())), preferred_element_type=F32
        )
    row = lax.broadcasted_iota(I32, (8, span), 0)
    for c in range(chips):
        part = total[:, c * span : (c + 1) * span]
        number = jnp.broadcast_to(offset[c : c + 1], (8, span))
        part = jnp.where(row == 0, number, jnp.where(row == 3, part + blocks, part))
        out_ref[c] = part[:4].astype(I32)


def tile_kernel(core, own_ref, other_ref, out_ref, buf, sems):
    held, _, width = own_ref.shape
    steps, step = buf.shape[:2]
    half = steps // 2
    mine = core[0]
    copies = [
        pltpu.make_async_copy(
            (own_ref if s < half else other_ref).at[pl.ds(s % half * step, step)],
            buf.at[s],
            sems.at[s],
        )
        for s in range(steps)
    ]
    for copy in copies:
        copy.start()
    for s in range(steps):
        copies[s].wait()
        start = (mine if s < half else 1 - mine) * held + s % half * step

        def one(i, _):
            hi, lo = split(buf[s, i])
            out_ref[start + i, :, :width] = hi
            out_ref[start + i, :, width:] = lo
            return 0

        lax.fori_loop(0, step, one, 0, unroll=4)


def gather_kernel(planes, place, own_ref, *refs):
    pieces, out_ref = refs[:-1], refs[-1]
    count, half, width = own_ref.shape
    quarter = count // 4
    blk = place[2]
    low = lanes((half, width)) < half
    zero = jnp.zeros((half, width), F32)

    def put(src, start, n):
        for i in range(n):
            x = src[i]
            hi = x.astype(BF16).astype(F32)
            lo = pltpu.roll(x - hi, half, 1)
            out_ref[start + i, 0 * half : 1 * half] = jnp.where(low, hi, lo).astype(BF16)
            out_ref[start + i, 1 * half : 2 * half] = jnp.where(low, lo, hi).astype(BF16)
            out_ref[start + i, 2 * half : 3 * half] = jnp.where(low, hi, zero).astype(BF16)
            out_ref[start + i, 3 * half : 4 * half] = jnp.where(low, zero, hi).astype(BF16)

    put(own_ref, blk * count, count)
    for k in range(1, planes):
        plane = lax.rem(blk - k + planes, planes)
        for p in range(4):
            put(pieces[(k - 1) * 4 + p], plane * count + place[3 + p] * quarter, quarter)


def entry_kernel(g, lists, tiles_ref, proj_ref, out_ref, acc):
    blocks, half, width = out_ref.shape
    acc[...] = jnp.zeros_like(acc)

    def multiply(base, n):
        terms = [
            jnp.dot(
                tiles_ref[lists[g, 1, base + u]],
                proj_ref[lists[g, 2, base + u]],
                preferred_element_type=F32,
            )
            for u in range(n)
        ]
        for u in range(n):
            acc[lists[g, 3, base + u]] += terms[u]

    def step(s, _):
        multiply(s * UNROLL, UNROLL)
        return 0

    number = lists[g, 0, 0]
    steps = (number + UNROLL // 2 - 1) // UNROLL
    lax.fori_loop(0, steps, step, 0)

    @pl.when(number > steps * UNROLL)
    def _():
        multiply(steps * UNROLL, UNROLL // 2)

    low = lanes((half, width)) < half
    for i in range(blocks):
        top, bottom = acc[i, :half], acc[i, half:]
        a, b = jnp.where(low, top, bottom), jnp.where(low, bottom, top)
        out_ref[i] = a + pltpu.roll(b, half, 1)


def final_kernel(place, left_ref, own_a, own_b, own_c, other, out_ref):
    blocks, _, _ = own_a.shape
    keep_first = place[1] == 0
    for i in range(blocks):
        own = own_a[i] + own_b[i] + own_c[i]
        first = jnp.where(keep_first, own, other[i])
        second = jnp.where(keep_first, other[i], own)
        top, bottom = unfold_halves(first, second)
        summed = jnp.concatenate([top, bottom], axis=0)
        out_ref[i] = triple(left_ref[i], summed, ((1,), (0,)))


def call(kernel, prefetch, ins, out, scratch, args, estimate, limit, grid=(), out_spec=VMEM):
    return pl.pallas_call(
        kernel,
        out_shape=out,
        grid_spec=pltpu.PrefetchScalarGridSpec(
            num_scalar_prefetch=prefetch,
            grid=grid,
            in_specs=ins,
            out_specs=out_spec,
            scratch_shapes=scratch,
        ),
        compiler_params=pltpu.CompilerParams(vmem_limit_bytes=limit),
        cost_estimate=estimate,
    )(*args)


def work(
    vectors, left, right, tiles, pair_cols, pair_owner, pair_slot, pair_counts
):
    rows, planes = lax.axis_size("rows"), lax.axis_size("blk")
    row, blk = lax.axis_index("rows"), lax.axis_index("blk")
    blocks, fine, coarse = left.shape
    vecs = vectors.shape[1]
    count = right.shape[0]
    held = tiles.shape[0]
    listed = pair_cols.shape[1]
    chips = rows // 2
    bits = chips.bit_length() - 1
    cap = blocks * listed // chips
    half = coarse // 2
    quarter = count // 4
    core, chip = row & 1, row >> 1
    b0, b1 = chip & 1, (chip >> 1) & 1
    part = blk & 1

    def physical(mask, core_at):
        return mask if core_at == 0 else (mask & ~3) | ((mask & 1) << 1) | ((mask >> 1) & 1)

    def across(mask):
        return [(r, r ^ (physical(mask, r % 2) << 1)) for r in range(rows)]

    def swap(x):
        return lax.ppermute(x, "rows", [(r, r ^ 1) for r in range(rows)])

    def turn(x, k):
        return lax.ppermute(x, "blk", [(b, (b + k) % planes) for b in range(planes)])

    def mate(x):
        return lax.ppermute(x, "blk", [(b, b ^ 1) for b in range(planes)])

    mine = jnp.where(core == 0, b0, 2 + b1)
    theirs = jnp.where(core == 0, 2 + b1, b0)
    place = jnp.stack([mine, part, blk, mine, mine ^ 1, theirs, theirs ^ 1]).astype(I32)

    v = vectors.reshape(count, fine, vecs)
    v, right = in_hbm(v), in_hbm(right)

    def blocks_of(n):
        return [pltpu.VMEM((n, fine, vecs), F32)] * 2 + [pltpu.SemaphoreType.DMA((2,))]

    sent = call(
        send_kernel, 1, [HBM, HBM],
        jax.ShapeDtypeStruct((2, quarter, half, vecs), F32),
        blocks_of(quarter), (place, v, right),
        cost(2 * quarter * 128**3 * 3, 2 * quarter * 65536), 8 * MIB,
    )
    arrived = {k: turn(sent[k % 2], k) for k in range(1, planes)}
    other_tiles = swap(tiles)

    span = pl.cdiv(cap, 128) * 128
    lists = call(
        functools.partial(list_kernel, chips, held), 0, [HBM] * 4,
        jax.ShapeDtypeStruct((chips, 4, span), I32),
        [
            pltpu.VMEM((3, blocks, listed), I32),
            pltpu.SMEM((blocks,), I32),
            pltpu.SemaphoreType.DMA((4,)),
        ],
        (in_hbm(pair_cols), in_hbm(pair_owner), in_hbm(pair_slot), in_hbm(pair_counts)),
        cost(10**8, 16384), 8 * MIB,
    )
    gathered = jnp.stack([lists, mate(lists)], axis=1)
    tables = {}
    for m in range(chips):
        to_chip = chip ^ jnp.where(core == 0, physical(m, 0), physical(m, 1))
        chosen = lax.dynamic_index_in_dim(gathered, to_chip, 0, keepdims=False)
        tables[m] = chosen if m == 0 else lax.ppermute(chosen, "rows", across(m))

    own = call(
        own_kernel, 1, [HBM, HBM],
        jax.ShapeDtypeStruct((count, half, vecs), F32),
        blocks_of(count), (place, v, right), cost(2 * count * 128**3 * 3, 2 * count * 65536), 8 * MIB,
    )
    packed = call(
        tile_kernel, 1, [HBM, HBM],
        jax.ShapeDtypeStruct((2 * held, coarse, 2 * coarse), BF16),
        [pltpu.VMEM((held // 4, 8, coarse, coarse), F32), pltpu.SemaphoreType.DMA((held // 4,))],
        (core.reshape(1).astype(I32), in_hbm(tiles), in_hbm(other_tiles)),
        cost(held * 65536 * 4, held * 65536 * 4), 2 * held * 65536 + 4 * MIB,
    )

    pieces = []
    for k in range(1, planes):
        z = arrived[k]
        x = lax.ppermute(z, "rows", across(1))
        pieces += [z, x, swap(z), swap(x)]
    proj = call(
        functools.partial(gather_kernel, planes), 1, [VMEM] * (1 + len(pieces)),
        jax.ShapeDtypeStruct((planes * count, 2 * coarse, vecs), BF16),
        [], (place, own, *pieces), cost(10**6, 3 * planes * count * 32768), 16 * MIB,
    )

    def partial_sum(m, g):
        return call(
            functools.partial(entry_kernel, g), 1, [VMEM, VMEM],
            jax.ShapeDtypeStruct((blocks, half, vecs), F32),
            [pltpu.VMEM((blocks + 1, coarse, vecs), F32)],
            (tables[m], packed, proj),
            cost(cap * 128**3 * 4, 4 * MIB), 12 * MIB,
        )

    def reduce_over_chips(g):
        total = {m: [partial_sum(m, g)] for m in range(chips)}
        for j in range(bits):
            bit = 1 << j
            for m in sorted((m for m in range(chips) if m & bit and not m & (bit - 1)), reverse=True):
                value = functools.reduce(jnp.add, total[m])
                total[m ^ bit].append(lax.ppermute(value, "rows", across(bit)))
        return total[0]

    other = functools.reduce(jnp.add, reduce_over_chips(1))
    other = mate(other)
    sums = reduce_over_chips(0)
    while len(sums) > 3:
        sums = [sums[0] + sums[1]] + sums[2:]
    result = call(
        final_kernel, 1, [VMEM] * 5,
        jax.ShapeDtypeStruct((blocks, fine, vecs), F32),
        [], (place, left, *sums, other), cost(2 * blocks * 128**3 * 3, 2 * MIB), 8 * MIB,
    )
    return result.reshape(blocks * fine, vecs)


def solution(mesh):
    return jax.shard_map(
        work,
        mesh=mesh,
        in_specs=(
            P("blk", None),
            P(("rows", "blk"), None, None),
            P("blk", None, None),
            P("rows", None, None),
            P(("rows", "blk"), None),
            P(("rows", "blk"), None),
            P(("rows", "blk"), None),
            P(("rows", "blk")),
        ),
        out_specs=P(("rows", "blk"), None),
        check_vma=False,
    )
```

```python
import functools

import jax
import jax.numpy as jnp
from jax import lax
from jax.experimental import pallas as pl
from jax.experimental.pallas import tpu as pltpu
from jax.sharding import PartitionSpec as P


F32 = jnp.float32
BF16 = jnp.bfloat16
I32 = jnp.int32
UNROLL = 16
MIB = 1 << 20


VMEM = pl.BlockSpec(memory_space=pltpu.VMEM)
HBM = pl.BlockSpec(memory_space=pltpu.HBM)


def in_hbm(x):
    return pltpu.with_memory_space_constraint(x, pltpu.HBM)


def cost(flops, nbytes):
    return pl.CostEstimate(flops=flops, bytes_accessed=nbytes, transcendentals=0)


def split(x):
    hi = x.astype(BF16)
    return hi, (x - hi.astype(F32)).astype(BF16)


def lanes(shape):
    return lax.broadcasted_iota(I32, shape, len(shape) - 1)


def triple(a, b, dims):
    a_hi, a_lo = split(a)
    b_hi, b_lo = split(b)

    def dot(x, y):
        return lax.dot_general(x, y, (dims, ((), ())), preferred_element_type=F32)

    return dot(a_hi, b_hi) + dot(a_hi, b_lo) + dot(a_lo, b_hi)


def project_kernel(place, v_ref, r_ref, out_ref, v_buf, r_buf, sems):
    count = v_buf.shape[0]
    first = place[0] * count if count < v_ref.shape[0] else 0
    copies = [
        pltpu.make_async_copy(ref.at[pl.ds(first, count)], buf, sems.at[i])
        for i, (ref, buf) in enumerate(((v_ref, v_buf), (r_ref, r_buf)))
    ]
    for copy in copies:
        copy.start()
    for copy in copies:
        copy.wait()
    for i in range(count):
        out_ref[i] = triple(r_buf[i], v_buf[i], ((0,), (0,)))


def list_kernel(chips, held, columns, cols, owner, slot, number, out_ref, words, counts, sems):
    blocks, listed = cols.shape
    span = out_ref.shape[2]
    copies = [
        pltpu.make_async_copy(ref, words.at[i], sems.at[i])
        for i, ref in enumerate((cols, owner, slot))
    ]
    copies += [pltpu.make_async_copy(number, counts, sems.at[3])]
    for copy in copies:
        copy.start()
    for copy in copies:
        copy.wait()
    kinds = lax.broadcasted_iota(I32, (16, listed), 0)
    upto = lax.broadcasted_iota(I32, (listed, listed), 0) <= lanes((listed, listed))
    upto = upto.astype(F32).astype(BF16)
    spots = lax.broadcasted_iota(I32, (chips * span, listed), 0).astype(F32)
    offset = jnp.zeros((16, 1), F32)
    total = jnp.zeros((8, chips * span), F32)
    for i in range(blocks):
        col, own, place = words[0, i : i + 1], words[1, i : i + 1], words[2, i : i + 1]
        chip = jnp.where(lanes((1, listed)) < counts[i], own >> 1, chips)
        match = (kinds == chip).astype(F32)
        ranks = jnp.dot(match.astype(BF16), upto, preferred_element_type=F32) + offset
        offset = offset + jnp.sum(match, axis=1, keepdims=True)
        rank = jnp.sum(match * ranks, axis=0, keepdims=True) - 1
        target = jnp.where(chip < chips, chip.astype(F32) * span + rank, -1.0)
        chosen = (spots == target).astype(F32).astype(BF16)
        one = jnp.ones((1, listed), F32)
        fields = jnp.concatenate(
            [
                one,
                ((own & 1) * held + place).astype(F32),
                (col - columns).astype(F32),
                one * i,
                jnp.zeros((4, listed), F32),
            ],
            axis=0,
        )
        total += lax.dot_general(
            fields.astype(BF16), chosen, (((1,), (1,)), ((), ())), preferred_element_type=F32
        )
    row = lax.broadcasted_iota(I32, (8, span), 0)
    for c in range(chips):
        part = total[:, c * span : (c + 1) * span]
        number = jnp.broadcast_to(offset[c : c + 1], (8, span))
        part = jnp.where(row == 0, number, jnp.where(row == 2, part + columns, part))
        out_ref[c] = part[:4].astype(I32)


def tile_kernel(core, own_ref, other_ref, out_ref, buf, sems):
    held, _, width = own_ref.shape
    steps, step = buf.shape[:2]
    half = steps // 2
    mine = core[0]
    copies = [
        pltpu.make_async_copy(
            (own_ref if s < half else other_ref).at[pl.ds(s % half * step, step)],
            buf.at[s],
            sems.at[s],
        )
        for s in range(steps)
    ]
    for copy in copies:
        copy.start()
    for s in range(steps):
        copies[s].wait()
        start = (mine if s < half else 1 - mine) * held + s % half * step

        def one(i, _):
            hi, lo = split(buf[s, i])
            out_ref[start + i, :, :width] = hi
            out_ref[start + i, :, width:] = lo
            return 0

        lax.fori_loop(0, step, one, 0, unroll=4)


def gather_kernel(planes, place, own_ref, *refs):
    pieces, out_ref = refs[:-1], refs[-1]
    count, _, width = own_ref.shape
    quarter = count // 4
    blk = place[1]
    out_ref[planes * count] = jnp.zeros_like(out_ref[planes * count])

    def put(src, start, n):
        for i in range(n):
            hi, lo = split(src[i])
            out_ref[start + i, :, :width] = hi
            out_ref[start + i, :, width:] = lo

    put(own_ref, blk * count, count)
    for k in range(1, planes):
        plane = lax.rem(blk - k + planes, planes)
        for p in range(4):
            put(pieces[(k - 1) * 4 + p], plane * count + place[2 + p] * quarter, quarter)


def entry_kernel(lists, tiles_ref, proj_ref, out_ref):
    _, _, width = out_ref.shape
    out_ref[...] = jnp.zeros_like(out_ref)

    def multiply(base, n):
        terms = []
        for u in range(n):
            proj = proj_ref[lists[2, base + u]]
            d = jnp.dot(
                tiles_ref[lists[1, base + u]],
                jnp.concatenate([proj, proj], axis=0),
                preferred_element_type=F32,
            )
            terms.append(d[:, :width] + d[:, width:])
        for u in range(n):
            out_ref[lists[3, base + u]] += terms[u]

    def step(s, _):
        multiply(s * UNROLL, UNROLL)
        return 0

    number = lists[0, 0]
    steps = (number + UNROLL // 2 - 1) // UNROLL
    lax.fori_loop(0, steps, step, 0)

    @pl.when(number > steps * UNROLL)
    def _():
        multiply(steps * UNROLL, UNROLL // 2)


def final_kernel(left_ref, *refs):
    sums, out_ref = refs[:-1], refs[-1]
    for i in range(out_ref.shape[0]):
        total = functools.reduce(jnp.add, [r[i] for r in sums])
        out_ref[i] = triple(left_ref[i], total, ((1,), (0,)))


def call(kernel, prefetch, ins, out, scratch, args, estimate, limit, grid=(), out_spec=VMEM):
    return pl.pallas_call(
        kernel,
        out_shape=out,
        grid_spec=pltpu.PrefetchScalarGridSpec(
            num_scalar_prefetch=prefetch,
            grid=grid,
            in_specs=ins,
            out_specs=out_spec,
            scratch_shapes=scratch,
        ),
        compiler_params=pltpu.CompilerParams(vmem_limit_bytes=limit),
        cost_estimate=estimate,
    )(*args)


def work(
    vectors, left, right, tiles, pair_cols, pair_owner, pair_slot, pair_counts
):
    rows, planes = lax.axis_size("rows"), lax.axis_size("blk")
    row, blk = lax.axis_index("rows"), lax.axis_index("blk")
    blocks, fine, coarse = left.shape
    vecs = vectors.shape[1]
    count = right.shape[0]
    held = tiles.shape[0]
    listed = pair_cols.shape[1]
    chips = rows // 2
    cap = blocks * listed // chips
    quarter = count // 4
    core, chip = row & 1, row >> 1
    b0, b1 = chip & 1, (chip >> 1) & 1

    def physical(mask, core_at):
        return mask if core_at == 0 else (mask & ~3) | ((mask & 1) << 1) | ((mask >> 1) & 1)

    def across(mask):
        return [(r, r ^ (physical(mask, r % 2) << 1)) for r in range(rows)]

    def swap(x):
        return lax.ppermute(x, "rows", [(r, r ^ 1) for r in range(rows)])

    def turn(x, k):
        return lax.ppermute(x, "blk", [(b, (b + k) % planes) for b in range(planes)])

    mine = jnp.where(core == 0, b0, 2 + b1)
    theirs = jnp.where(core == 0, 2 + b1, b0)
    place = jnp.stack([mine, blk, mine, mine ^ 1, theirs, theirs ^ 1]).astype(I32)

    v = vectors.reshape(count, fine, vecs)
    v, right = in_hbm(v), in_hbm(right)

    def project(n):
        return call(
            project_kernel, 1, [HBM, HBM],
            jax.ShapeDtypeStruct((n, coarse, vecs), F32),
            [pltpu.VMEM((n, fine, vecs), F32)] * 2 + [pltpu.SemaphoreType.DMA((2,))],
            (place, v, right), cost(2 * n * 128**3 * 3, 2 * n * 65536), 8 * MIB,
        )

    sent = project(quarter)
    arrived = {k: turn(sent, k) for k in range(1, planes)}
    other_tiles = swap(tiles)

    span = pl.cdiv(cap, 128) * 128
    lists = call(
        functools.partial(list_kernel, chips, held, planes * count), 0, [HBM] * 4,
        jax.ShapeDtypeStruct((chips, 4, span), I32),
        [
            pltpu.VMEM((3, blocks, listed), I32),
            pltpu.SMEM((blocks,), I32),
            pltpu.SemaphoreType.DMA((4,)),
        ],
        (in_hbm(pair_cols), in_hbm(pair_owner), in_hbm(pair_slot), in_hbm(pair_counts)),
        cost(10**8, 16384), 8 * MIB,
    )
    tables = {}
    for m in range(chips):
        to_chip = chip ^ jnp.where(core == 0, physical(m, 0), physical(m, 1))
        chosen = lax.dynamic_index_in_dim(lists, to_chip, 0, keepdims=False)
        tables[m] = chosen if m == 0 else lax.ppermute(chosen, "rows", across(m))

    own = project(count)
    packed = call(
        tile_kernel, 1, [HBM, HBM],
        jax.ShapeDtypeStruct((2 * held, coarse, 2 * coarse), BF16),
        [pltpu.VMEM((held // 4, 8, coarse, coarse), F32), pltpu.SemaphoreType.DMA((held // 4,))],
        (core.reshape(1).astype(I32), in_hbm(tiles), in_hbm(other_tiles)),
        cost(held * 65536 * 4, held * 65536 * 4), 2 * held * 65536 + 4 * MIB,
    )

    pieces = []
    for k in range(1, planes):
        z = arrived[k]
        x = lax.ppermute(z, "rows", across(1))
        pieces += [z, x, swap(z), swap(x)]
    proj = call(
        functools.partial(gather_kernel, planes), 1, [VMEM] * (1 + len(pieces)),
        jax.ShapeDtypeStruct((planes * count + 1, coarse, 2 * vecs), BF16),
        [], (place, own, *pieces), cost(10**6, 3 * planes * count * 32768), 16 * MIB,
    )

    total = {
        m: [
            call(
                entry_kernel, 1, [VMEM, VMEM],
                jax.ShapeDtypeStruct((blocks, coarse, vecs), F32),
                [], (tables[m], packed, proj),
                cost(cap * 128**3 * 8, 4 * MIB), 12 * MIB,
            )
        ]
        for m in range(chips)
    }
    for m in masks_of(chips):
        bit = m & -m
        value = functools.reduce(jnp.add, total[m])
        total[m ^ bit].append(lax.ppermute(value, "rows", across(bit)))
    result = call(
        final_kernel, 0, [VMEM] * (1 + len(total[0])),
        jax.ShapeDtypeStruct((blocks, fine, vecs), F32),
        [], (left, *total[0]), cost(2 * blocks * 128**3 * 3, 2 * MIB), 8 * MIB,
    )
    return result.reshape(blocks * fine, vecs)


def masks_of(chips):
    return sorted(range(1, chips), key=lambda m: (m & -m, -m))


def solution(mesh):
    return jax.shard_map(
        work,
        mesh=mesh,
        in_specs=(
            P("blk", None),
            P(("rows", "blk"), None, None),
            P("blk", None, None),
            P("rows", None, None),
            P(("rows", "blk"), None),
            P(("rows", "blk"), None),
            P(("rows", "blk"), None),
            P(("rows", "blk")),
        ),
        out_specs=P(("rows", "blk"), None),
        check_vma=False,
    )
```

```python
import functools

import jax
import jax.numpy as jnp
from jax import lax
from jax.experimental import pallas as pl
from jax.experimental.pallas import tpu as pltpu
from jax.sharding import PartitionSpec as P


F32 = jnp.float32
BF16 = jnp.bfloat16
I32 = jnp.int32
UNROLL = 16
MIB = 1 << 20


VMEM = pl.BlockSpec(memory_space=pltpu.VMEM)
HBM = pl.BlockSpec(memory_space=pltpu.HBM)


def in_hbm(x):
    return pltpu.with_memory_space_constraint(x, pltpu.HBM)


def cost(flops, nbytes):
    return pl.CostEstimate(flops=flops, bytes_accessed=nbytes, transcendentals=0)


def split(x):
    hi = x.astype(BF16)
    return hi, (x - hi.astype(F32)).astype(BF16)


def lanes(shape):
    return lax.broadcasted_iota(I32, shape, len(shape) - 1)


def triple(a, b, dims):
    a_hi, a_lo = split(a)
    b_hi, b_lo = split(b)

    def dot(x, y):
        return lax.dot_general(x, y, (dims, ((), ())), preferred_element_type=F32)

    return dot(a_hi, b_hi) + dot(a_hi, b_lo) + dot(a_lo, b_hi)


def project_kernel(place, v_ref, r_ref, out_ref, *rest):
    v_buf, r_buf, sems = rest[-3:]
    count = v_buf.shape[0]
    first = place[0] * count if count < v_ref.shape[0] else 0
    copies = [
        pltpu.make_async_copy(ref.at[pl.ds(first, count)], buf, sems.at[i])
        for i, (ref, buf) in enumerate(((v_ref, v_buf), (r_ref, r_buf)))
    ]
    for copy in copies:
        copy.start()
    for copy in copies:
        copy.wait()
    for i in range(count):
        out_ref[i] = triple(r_buf[i], v_buf[i], ((0,), (0,)))
        for half_ref in rest[:-3]:
            rows = half_ref.shape[1]
            half_ref[i] = out_ref[i, pl.ds(pl.multiple_of(place[6] * rows, rows), rows)]


def list_kernel(chips, held, columns, cols, owner, slot, number, out_ref, words, counts, sems):
    blocks, listed = cols.shape
    span = out_ref.shape[2]
    copies = [
        pltpu.make_async_copy(ref, words.at[i], sems.at[i])
        for i, ref in enumerate((cols, owner, slot))
    ]
    copies += [pltpu.make_async_copy(number, counts, sems.at[3])]
    for copy in copies:
        copy.start()
    for copy in copies:
        copy.wait()
    kinds = lax.broadcasted_iota(I32, (16, listed), 0)
    upto = lax.broadcasted_iota(I32, (listed, listed), 0) <= lanes((listed, listed))
    upto = upto.astype(F32).astype(BF16)
    spots = lax.broadcasted_iota(I32, (chips * span, listed), 0).astype(F32)
    offset = jnp.zeros((16, 1), F32)
    total = jnp.zeros((8, chips * span), F32)
    for i in range(blocks):
        col, own, place = words[0, i : i + 1], words[1, i : i + 1], words[2, i : i + 1]
        chip = jnp.where(lanes((1, listed)) < counts[i], own >> 1, chips)
        match = (kinds == chip).astype(F32)
        ranks = jnp.dot(match.astype(BF16), upto, preferred_element_type=F32) + offset
        offset = offset + jnp.sum(match, axis=1, keepdims=True)
        rank = jnp.sum(match * ranks, axis=0, keepdims=True) - 1
        target = jnp.where(chip < chips, chip.astype(F32) * span + rank, -1.0)
        chosen = (spots == target).astype(F32).astype(BF16)
        one = jnp.ones((1, listed), F32)
        fields = jnp.concatenate(
            [
                one,
                ((own & 1) * held + place).astype(F32),
                (col - columns).astype(F32),
                one * i,
                jnp.zeros((4, listed), F32),
            ],
            axis=0,
        )
        total += lax.dot_general(
            fields.astype(BF16), chosen, (((1,), (1,)), ((), ())), preferred_element_type=F32
        )
    row = lax.broadcasted_iota(I32, (8, span), 0)
    for c in range(chips):
        part = total[:, c * span : (c + 1) * span]
        number = jnp.broadcast_to(offset[c : c + 1], (8, span))
        part = jnp.where(row == 0, number, jnp.where(row == 2, part + columns, part))
        out_ref[c] = part[:4].astype(I32)


def tile_kernel(core, own_ref, other_ref, out_ref, buf, sems):
    held, _, width = own_ref.shape
    steps, step = buf.shape[:2]
    half = steps // 2
    mine = core[0]
    copies = [
        pltpu.make_async_copy(
            (own_ref if s < half else other_ref).at[pl.ds(s % half * step, step)],
            buf.at[s],
            sems.at[s],
        )
        for s in range(steps)
    ]
    for copy in copies:
        copy.start()
    for s in range(steps):
        copies[s].wait()
        start = (mine if s < half else 1 - mine) * held + s % half * step

        def one(i, _):
            hi, lo = split(buf[s, i])
            out_ref[start + i, :, :width] = hi
            out_ref[start + i, :, width:] = lo
            return 0

        lax.fori_loop(0, step, one, 0, unroll=4)


def gather_kernel(planes, place, own_ref, *refs):
    pieces, out_ref = refs[:-1], refs[-1]
    count, _, width = own_ref.shape
    quarter = count // 4
    blk = place[1]
    out_ref[planes * count] = jnp.zeros_like(out_ref[planes * count])

    def put(src, start, first_row):
        rows = pl.ds(first_row, src.shape[1])
        for i in range(src.shape[0]):
            hi, lo = split(src[i])
            out_ref[start + i, rows, :width] = hi
            out_ref[start + i, rows, width:] = lo

    put(own_ref, blk * count, 0)
    at = 0
    for k in range(1, planes):
        start = lax.rem(blk - k + planes, planes) * count
        if k != planes // 2:
            for p in range(4):
                put(pieces[at + p], start + place[2 + p] * quarter, 0)
            at += 4
            continue
        for p in range(4):
            half = place[6 + p // 2]
            rows = pieces[at].shape[1]
            for side in range(2):
                row = pl.multiple_of((half if side == 0 else 1 - half) * rows, rows)
                put(pieces[at + 2 * p + side], start + place[2 + p] * quarter, row)
        at += 8


def entry_kernel(lists, tiles_ref, proj_ref, out_ref):
    _, _, width = out_ref.shape
    out_ref[...] = jnp.zeros_like(out_ref)

    def multiply(base, n):
        terms = []
        for u in range(n):
            proj = proj_ref[lists[2, base + u]]
            d = jnp.dot(
                tiles_ref[lists[1, base + u]],
                jnp.concatenate([proj, proj], axis=0),
                preferred_element_type=F32,
            )
            terms.append(d[:, :width] + d[:, width:])
        for u in range(n):
            out_ref[lists[3, base + u]] += terms[u]

    def step(s, _):
        multiply(s * UNROLL, UNROLL)
        return 0

    number = lists[0, 0]
    steps = (number + UNROLL // 2 - 1) // UNROLL
    lax.fori_loop(0, steps, step, 0)

    @pl.when(number > steps * UNROLL)
    def _():
        multiply(steps * UNROLL, UNROLL // 2)


def final_kernel(left_ref, *refs):
    sums, out_ref = refs[:-1], refs[-1]
    for i in range(out_ref.shape[0]):
        total = functools.reduce(jnp.add, [r[i] for r in sums])
        out_ref[i] = triple(left_ref[i], total, ((1,), (0,)))


def call(kernel, prefetch, ins, out, scratch, args, estimate, limit, grid=(), out_spec=VMEM):
    return pl.pallas_call(
        kernel,
        out_shape=out,
        grid_spec=pltpu.PrefetchScalarGridSpec(
            num_scalar_prefetch=prefetch,
            grid=grid,
            in_specs=ins,
            out_specs=out_spec,
            scratch_shapes=scratch,
        ),
        compiler_params=pltpu.CompilerParams(vmem_limit_bytes=limit),
        cost_estimate=estimate,
    )(*args)


def work(
    vectors, left, right, tiles, pair_cols, pair_owner, pair_slot, pair_counts
):
    rows, planes = lax.axis_size("rows"), lax.axis_size("blk")
    row, blk = lax.axis_index("rows"), lax.axis_index("blk")
    blocks, fine, coarse = left.shape
    vecs = vectors.shape[1]
    count = right.shape[0]
    held = tiles.shape[0]
    listed = pair_cols.shape[1]
    chips = rows // 2
    cap = blocks * listed // chips
    quarter = count // 4
    core, chip = row & 1, row >> 1
    b0, b1 = chip & 1, (chip >> 1) & 1

    def physical(mask, core_at):
        return mask if core_at == 0 else (mask & ~3) | ((mask & 1) << 1) | ((mask >> 1) & 1)

    def across(mask):
        return [(r, r ^ (physical(mask, r % 2) << 1)) for r in range(rows)]

    def swap(x):
        return lax.ppermute(x, "rows", [(r, r ^ 1) for r in range(rows)])

    def turn(x, k):
        return lax.ppermute(x, "blk", [(b, (b + k) % planes) for b in range(planes)])

    mine = jnp.where(core == 0, b0, 2 + b1)
    theirs = jnp.where(core == 0, 2 + b1, b0)
    row_half = jnp.where(core == 0, b1, b0)
    their_half = jnp.where(core == 0, b0, b1)
    place = jnp.stack([mine, blk, mine, mine ^ 1, theirs, theirs ^ 1, row_half, their_half]).astype(I32)

    v = vectors.reshape(count, fine, vecs)
    v, right = in_hbm(v), in_hbm(right)

    def project(n, out):
        return call(
            project_kernel, 1, [HBM, HBM], out,
            [pltpu.VMEM((n, fine, vecs), F32)] * 2 + [pltpu.SemaphoreType.DMA((2,))],
            (place, v, right), cost(2 * n * 128**3 * 3, 2 * n * 65536), 8 * MIB,
            out_spec=[VMEM] * len(out) if isinstance(out, list) else VMEM,
        )

    middle = planes // 2
    sent, sent_half = project(
        quarter,
        [
            jax.ShapeDtypeStruct((quarter, coarse, vecs), F32),
            jax.ShapeDtypeStruct((quarter, coarse // 2, vecs), F32),
        ],
    )
    arrived = {k: turn(sent_half if k == middle else sent, k) for k in range(1, planes)}
    other_tiles = swap(tiles)

    span = pl.cdiv(cap, 128) * 128
    lists = call(
        functools.partial(list_kernel, chips, held, planes * count), 0, [HBM] * 4,
        jax.ShapeDtypeStruct((chips, 4, span), I32),
        [
            pltpu.VMEM((3, blocks, listed), I32),
            pltpu.SMEM((blocks,), I32),
            pltpu.SemaphoreType.DMA((4,)),
        ],
        (in_hbm(pair_cols), in_hbm(pair_owner), in_hbm(pair_slot), in_hbm(pair_counts)),
        cost(10**8, 16384), 8 * MIB,
    )
    tables = {}
    for m in range(chips):
        to_chip = chip ^ jnp.where(core == 0, physical(m, 0), physical(m, 1))
        chosen = lax.dynamic_index_in_dim(lists, to_chip, 0, keepdims=False)
        tables[m] = chosen if m == 0 else lax.ppermute(chosen, "rows", across(m))

    own = project(count, jax.ShapeDtypeStruct((count, coarse, vecs), F32))
    packed = call(
        tile_kernel, 1, [HBM, HBM],
        jax.ShapeDtypeStruct((2 * held, coarse, 2 * coarse), BF16),
        [pltpu.VMEM((held // 4, 8, coarse, coarse), F32), pltpu.SemaphoreType.DMA((held // 4,))],
        (core.reshape(1).astype(I32), in_hbm(tiles), in_hbm(other_tiles)),
        cost(held * 65536 * 4, held * 65536 * 4), 2 * held * 65536 + 4 * MIB,
    )

    def spread(x, mask=1):
        return lax.ppermute(x, "rows", across(mask))

    pieces = []
    for k in range(1, planes):
        z = arrived[k]
        if k == middle:
            rest = spread(z, 2)
            x, x_rest = spread(z), spread(rest)
            pieces += [z, rest, x, x_rest, swap(z), swap(rest)]
            pieces += [swap(x), swap(x_rest)]
        else:
            x = spread(z)
            pieces += [z, x, swap(z), swap(x)]
    proj = call(
        functools.partial(gather_kernel, planes), 1, [VMEM] * (1 + len(pieces)),
        jax.ShapeDtypeStruct((planes * count + 1, coarse, 2 * vecs), BF16),
        [], (place, own, *pieces), cost(10**6, 3 * planes * count * 32768), 16 * MIB,
    )

    total = {
        m: [
            call(
                entry_kernel, 1, [VMEM, VMEM],
                jax.ShapeDtypeStruct((blocks, coarse, vecs), F32),
                [], (tables[m], packed, proj),
                cost(cap * 128**3 * 8, 4 * MIB), 12 * MIB,
            )
        ]
        for m in range(chips)
    }
    for m in masks_of(chips):
        bit = m & -m
        value = functools.reduce(jnp.add, total[m])
        total[m ^ bit].append(lax.ppermute(value, "rows", across(bit)))
    result = call(
        final_kernel, 0, [VMEM] * (1 + len(total[0])),
        jax.ShapeDtypeStruct((blocks, fine, vecs), F32),
        [], (left, *total[0]), cost(2 * blocks * 128**3 * 3, 2 * MIB), 8 * MIB,
    )
    return result.reshape(blocks * fine, vecs)


def masks_of(chips):
    return sorted(range(1, chips), key=lambda m: (m & -m, -m))


def solution(mesh):
    return jax.shard_map(
        work,
        mesh=mesh,
        in_specs=(
            P("blk", None),
            P(("rows", "blk"), None, None),
            P("blk", None, None),
            P("rows", None, None),
            P(("rows", "blk"), None),
            P(("rows", "blk"), None),
            P(("rows", "blk"), None),
            P(("rows", "blk")),
        ),
        out_specs=P(("rows", "blk"), None),
        check_vma=False,
    )
```

```python
import functools

import jax
import jax.numpy as jnp
from jax import lax
from jax.experimental import pallas as pl
from jax.experimental.pallas import tpu as pltpu
from jax.sharding import PartitionSpec as P


F32 = jnp.float32
BF16 = jnp.bfloat16
I32 = jnp.int32
UNROLL = 16
MIB = 1 << 20


VMEM = pl.BlockSpec(memory_space=pltpu.VMEM)
HBM = pl.BlockSpec(memory_space=pltpu.HBM)


def in_hbm(x):
    return pltpu.with_memory_space_constraint(x, pltpu.HBM)


def cost(flops, nbytes):
    return pl.CostEstimate(flops=flops, bytes_accessed=nbytes, transcendentals=0)


def split(x):
    hi = x.astype(BF16)
    return hi, (x - hi.astype(F32)).astype(BF16)


def lanes(shape):
    return lax.broadcasted_iota(I32, shape, len(shape) - 1)


def triple(a, b, dims):
    a_hi, a_lo = split(a)
    b_hi, b_lo = split(b)

    def dot(x, y):
        return lax.dot_general(x, y, (dims, ((), ())), preferred_element_type=F32)

    return dot(a_hi, b_hi) + dot(a_hi, b_lo) + dot(a_lo, b_hi)


def project_kernel(place, v_ref, r_ref, out_ref, *rest):
    v_buf, r_buf, sems = rest[-3:]
    count = v_buf.shape[0]
    first = place[0] * count if count < v_ref.shape[0] else 0
    copies = [
        pltpu.make_async_copy(ref.at[pl.ds(first, count)], buf, sems.at[i])
        for i, (ref, buf) in enumerate(((v_ref, v_buf), (r_ref, r_buf)))
    ]
    for copy in copies:
        copy.start()
    for copy in copies:
        copy.wait()
    for i in range(count):
        out_ref[i] = triple(r_buf[i], v_buf[i], ((0,), (0,)))
        for half_ref in rest[:-3]:
            rows = half_ref.shape[1]
            half_ref[i] = out_ref[i, pl.ds(pl.multiple_of(place[6] * rows, rows), rows)]


def list_kernel(chips, held, columns, cols, owner, slot, number, out_ref, words, counts, sems):
    blocks, listed = cols.shape
    span = out_ref.shape[1]
    copies = [
        pltpu.make_async_copy(ref, words.at[i], sems.at[i])
        for i, ref in enumerate((cols, owner, slot))
    ]
    copies += [pltpu.make_async_copy(number, counts, sems.at[3])]
    for copy in copies:
        copy.start()
    for copy in copies:
        copy.wait()
    kinds = lax.broadcasted_iota(I32, (16, listed), 0)
    upto = lax.broadcasted_iota(I32, (listed, listed), 0) <= lanes((listed, listed))
    upto = upto.astype(F32).astype(BF16)
    spots = lax.broadcasted_iota(I32, (chips * span, listed), 0).astype(F32)
    offset = jnp.zeros((16, 1), F32)
    total = jnp.zeros((8, chips * span), F32)
    for i in range(blocks):
        col, own, place = words[0, i : i + 1], words[1, i : i + 1], words[2, i : i + 1]
        chip = jnp.where(lanes((1, listed)) < counts[i], own >> 1, chips)
        match = (kinds == chip).astype(F32)
        ranks = jnp.dot(match.astype(BF16), upto, preferred_element_type=F32) + offset
        offset = offset + jnp.sum(match, axis=1, keepdims=True)
        rank = jnp.sum(match * ranks, axis=0, keepdims=True) - 1
        target = jnp.where(chip < chips, chip.astype(F32) * span + rank, -1.0)
        chosen = (spots == target).astype(F32).astype(BF16)
        one = jnp.ones((1, listed), F32)
        fields = jnp.concatenate(
            [
                one,
                ((own & 1) * held + place).astype(F32),
                (col - columns).astype(F32),
                one * i,
                jnp.zeros((4, listed), F32),
            ],
            axis=0,
        )
        total += lax.dot_general(
            fields.astype(BF16), chosen, (((1,), (1,)), ((), ())), preferred_element_type=F32
        )
    row = lax.broadcasted_iota(I32, (8, span), 0)
    for c in range(chips):
        part = total[:, c * span : (c + 1) * span]
        number = jnp.broadcast_to(offset[c : c + 1], (8, span))
        part = jnp.where(row == 0, number, jnp.where(row == 2, part + columns, part))
        out_ref[8 * c : 8 * c + 8] = part


def tile_kernel(core, own_ref, other_ref, out_ref, buf, sems):
    held, _, width = own_ref.shape
    steps, step = buf.shape[:2]
    half = steps // 2
    mine = core[0]
    copies = [
        pltpu.make_async_copy(
            (own_ref if s < half else other_ref).at[pl.ds(s % half * step, step)],
            buf.at[s],
            sems.at[s],
        )
        for s in range(steps)
    ]
    for copy in copies:
        copy.start()
    for s in range(steps):
        copies[s].wait()
        start = (mine if s < half else 1 - mine) * held + s % half * step

        def one(i, _):
            hi, lo = split(buf[s, i])
            out_ref[start + i, :, :width] = hi
            out_ref[start + i, :, width:] = lo
            return 0

        lax.fori_loop(0, step, one, 0, unroll=4)


def gather_kernel(planes, holders, place, own_ref, *refs):
    chips = len(holders)
    pieces, (out_ref, *table_refs) = refs[: -1 - chips], refs[-1 - chips :]
    for holder, table in zip(holders, table_refs):
        base = pieces[holder].shape[0] - 8 * chips
        table[...] = pieces[holder][pl.ds(pl.multiple_of(base + 8 * place[8], 8), 8)].astype(I32)
    count, _, width = own_ref.shape
    quarter = count // 4
    blk = place[1]
    out_ref[planes * count] = jnp.zeros_like(out_ref[planes * count])

    def put(src, start):
        for i in range(src.shape[0]):
            hi, lo = split(src[i])
            out_ref[start + i, :, :width] = hi
            out_ref[start + i, :, width:] = lo

    def put_rows(src, start, half):
        n = out_ref.shape[1] // 2
        rows = pl.ds(pl.multiple_of(half * n, n), n)
        for i in range(quarter):
            hi, lo = split(src[i * n : (i + 1) * n])
            out_ref[start + i, rows, :width] = hi
            out_ref[start + i, rows, width:] = lo

    put(own_ref, blk * count)
    at = 0
    for k in range(1, planes):
        start = lax.rem(blk - k + planes, planes) * count
        if k != planes // 2:
            for p in range(4):
                put(pieces[at + p], start + place[2 + p] * quarter)
            at += 4
            continue
        for p in range(4):
            half = place[6 + p // 2]
            to = start + place[2 + p] * quarter
            put_rows(pieces[at + 2 * p], to, half)
            put_rows(pieces[at + 2 * p + 1], to, 1 - half)
        at += 8


def entry_kernel(lists, tiles_ref, proj_ref, out_ref):
    _, _, width = out_ref.shape
    out_ref[...] = jnp.zeros_like(out_ref)

    def multiply(base, n):
        terms = []
        for u in range(n):
            proj = proj_ref[lists[2, base + u]]
            d = jnp.dot(
                tiles_ref[lists[1, base + u]],
                jnp.concatenate([proj, proj], axis=0),
                preferred_element_type=F32,
            )
            terms.append(d[:, :width] + d[:, width:])
        for u in range(n):
            out_ref[lists[3, base + u]] += terms[u]

    def step(s, _):
        multiply(s * UNROLL, UNROLL)
        return 0

    number = lists[0, 0]
    steps = (number + UNROLL // 2 - 1) // UNROLL
    lax.fori_loop(0, steps, step, 0)

    @pl.when(number > steps * UNROLL)
    def _():
        multiply(steps * UNROLL, UNROLL // 2)


def final_kernel(left_ref, *refs):
    sums, out_ref = refs[:-1], refs[-1]
    for i in range(out_ref.shape[0]):
        total = functools.reduce(jnp.add, [r[i] for r in sums])
        out_ref[i] = triple(left_ref[i], total, ((1,), (0,)))


def call(kernel, prefetch, ins, out, scratch, args, estimate, limit, grid=(), out_spec=VMEM):
    return pl.pallas_call(
        kernel,
        out_shape=out,
        grid_spec=pltpu.PrefetchScalarGridSpec(
            num_scalar_prefetch=prefetch,
            grid=grid,
            in_specs=ins,
            out_specs=out_spec,
            scratch_shapes=scratch,
        ),
        compiler_params=pltpu.CompilerParams(vmem_limit_bytes=limit),
        cost_estimate=estimate,
    )(*args)


def work(
    vectors, left, right, tiles, pair_cols, pair_owner, pair_slot, pair_counts
):
    rows, planes = lax.axis_size("rows"), lax.axis_size("blk")
    row, blk = lax.axis_index("rows"), lax.axis_index("blk")
    blocks, fine, coarse = left.shape
    vecs = vectors.shape[1]
    count = right.shape[0]
    held = tiles.shape[0]
    listed = pair_cols.shape[1]
    chips = rows // 2
    cap = blocks * listed // chips
    quarter = count // 4
    core, chip = row & 1, row >> 1
    b0, b1 = chip & 1, (chip >> 1) & 1

    def physical(mask, core_at):
        return mask if core_at == 0 else (mask & ~3) | ((mask & 1) << 1) | ((mask >> 1) & 1)

    def across(mask):
        return [(r, r ^ (physical(mask, r % 2) << 1)) for r in range(rows)]

    def swap(x):
        return lax.ppermute(x, "rows", [(r, r ^ 1) for r in range(rows)])

    def turn(x, k):
        return lax.ppermute(x, "blk", [(b, (b + k) % planes) for b in range(planes)])

    mine = jnp.where(core == 0, b0, 2 + b1)
    theirs = jnp.where(core == 0, 2 + b1, b0)
    row_half = jnp.where(core == 0, b1, b0)
    their_half = jnp.where(core == 0, b0, b1)
    place = jnp.stack([mine, blk, mine, mine ^ 1, theirs, theirs ^ 1, row_half, their_half, chip]).astype(I32)

    v = vectors.reshape(count, fine, vecs)
    v, right = in_hbm(v), in_hbm(right)

    def project(n, out):
        return call(
            project_kernel, 1, [HBM, HBM], out,
            [pltpu.VMEM((n, fine, vecs), F32)] * 2 + [pltpu.SemaphoreType.DMA((2,))],
            (place, v, right), cost(2 * n * 128**3 * 3, 2 * n * 65536), 8 * MIB,
            out_spec=[VMEM] * len(out) if isinstance(out, list) else VMEM,
        )

    middle = planes // 2
    sent, sent_half = project(
        quarter,
        [
            jax.ShapeDtypeStruct((quarter, coarse, vecs), F32),
            jax.ShapeDtypeStruct((quarter, coarse // 2, vecs), F32),
        ],
    )
    arrived = {k: turn(sent_half if k == middle else sent, k) for k in range(1, planes)}
    other_tiles = swap(tiles)

    span = pl.cdiv(cap, 128) * 128
    lists = call(
        functools.partial(list_kernel, chips, held, planes * count), 0, [HBM] * 4,
        jax.ShapeDtypeStruct((chips * 8, span), F32),
        [
            pltpu.VMEM((3, blocks, listed), I32),
            pltpu.SMEM((blocks,), I32),
            pltpu.SemaphoreType.DMA((4,)),
        ],
        (in_hbm(pair_cols), in_hbm(pair_owner), in_hbm(pair_slot), in_hbm(pair_counts)),
        cost(10**8, 16384), 8 * MIB,
    )
    own = project(count, jax.ShapeDtypeStruct((count, coarse, vecs), F32))
    packed = call(
        tile_kernel, 1, [HBM, pl.BlockSpec(memory_space=pl.ANY)],
        jax.ShapeDtypeStruct((2 * held, coarse, 2 * coarse), BF16),
        [pltpu.VMEM((held // 4, 8, coarse, coarse), F32), pltpu.SemaphoreType.DMA((held // 4,))],
        (core.reshape(1).astype(I32), in_hbm(tiles), other_tiles),
        cost(held * 65536 * 4, held * 65536 * 4), 2 * held * 65536 + 4 * MIB,
    )

    def spread(x, mask=1):
        return lax.ppermute(x, "rows", across(mask))

    pieces = []
    for k in range(1, planes):
        z = arrived[k]
        if k == middle:
            z = jnp.concatenate([z.reshape(-1, vecs), lists], axis=0)
            rest = spread(z, 2)
            x, x_rest = spread(z), spread(rest)
            ridden = {1: x, 2: rest, 3: x_rest}
            pieces += [z, rest, x, x_rest, swap(z), swap(rest)]
            pieces += [swap(x), swap(x_rest)]
        else:
            x = spread(z)
            pieces += [z, x, swap(z), swap(x)]

    holders = [len(pieces)] + [next(i for i, p in enumerate(pieces) if p is ridden[m]) for m in (1, 2, 3)]
    pieces += [lists]
    from_chip = [lists] + [ridden[m][-8 * chips :] for m in (1, 2, 3)]
    for bit in (1 << j for j in range(2, chips.bit_length() - 1)):
        for m in range(bit):
            from_chip.append(lax.ppermute(from_chip[m], "rows", across(bit)))
            holders.append(len(pieces))
            pieces.append(from_chip[-1])
    proj, *tables = call(
        functools.partial(gather_kernel, planes, holders), 1, [VMEM] * (1 + len(pieces)),
        [jax.ShapeDtypeStruct((planes * count + 1, coarse, 2 * vecs), BF16)]
        + [jax.ShapeDtypeStruct((8, span), I32)] * chips,
        [], (place, own, *pieces), cost(10**6, 3 * planes * count * 32768), 16 * MIB,
        out_spec=[VMEM] * (1 + chips),
    )

    total = {
        m: [
            call(
                entry_kernel, 1, [VMEM, VMEM],
                jax.ShapeDtypeStruct((blocks, coarse, vecs), F32),
                [], (tables[m], packed, proj),
                cost(cap * 128**3 * 8, 4 * MIB), 12 * MIB,
            )
        ]
        for m in range(chips)
    }
    for m in masks_of(chips):
        bit = m & -m
        value = functools.reduce(jnp.add, total[m])
        total[m ^ bit].append(lax.ppermute(value, "rows", across(bit)))
    result = call(
        final_kernel, 0, [VMEM] * (1 + len(total[0])),
        jax.ShapeDtypeStruct((blocks, fine, vecs), F32),
        [], (left, *total[0]), cost(2 * blocks * 128**3 * 3, 2 * MIB), 8 * MIB,
    )
    return result.reshape(blocks * fine, vecs)


def masks_of(chips):
    return sorted(range(1, chips), key=lambda m: (m & -m, -m))


def solution(mesh):
    return jax.shard_map(
        work,
        mesh=mesh,
        in_specs=(
            P("blk", None),
            P(("rows", "blk"), None, None),
            P("blk", None, None),
            P("rows", None, None),
            P(("rows", "blk"), None),
            P(("rows", "blk"), None),
            P(("rows", "blk"), None),
            P(("rows", "blk")),
        ),
        out_specs=P(("rows", "blk"), None),
        check_vma=False,
    )
```

```python
import functools

import jax
import jax.numpy as jnp
from jax import lax
from jax.experimental import pallas as pl
from jax.experimental.pallas import tpu as pltpu
from jax.sharding import PartitionSpec as P


F32 = jnp.float32
BF16 = jnp.bfloat16
I32 = jnp.int32
UNROLL = 16
MIB = 1 << 20


VMEM = pl.BlockSpec(memory_space=pltpu.VMEM)
HBM = pl.BlockSpec(memory_space=pltpu.HBM)


def in_hbm(x):
    return pltpu.with_memory_space_constraint(x, pltpu.HBM)


def cost(flops, nbytes):
    return pl.CostEstimate(flops=flops, bytes_accessed=nbytes, transcendentals=0)


def split(x):
    hi = x.astype(BF16)
    return hi, (x - hi.astype(F32)).astype(BF16)


def lanes(shape):
    return lax.broadcasted_iota(I32, shape, len(shape) - 1)


def triple(a, b, dims):
    a_hi, a_lo = split(a)
    b_hi, b_lo = split(b)

    def dot(x, y):
        return lax.dot_general(x, y, (dims, ((), ())), preferred_element_type=F32)

    return dot(a_hi, b_hi) + dot(a_hi, b_lo) + dot(a_lo, b_hi)


def project_kernel(place, v_ref, r_ref, out_ref, *rest):
    v_buf, r_buf, sems = rest[-3:]
    count = v_buf.shape[0]
    first = place[0] * count if count < v_ref.shape[0] else 0
    copies = [
        pltpu.make_async_copy(ref.at[pl.ds(first, count)], buf, sems.at[i])
        for i, (ref, buf) in enumerate(((v_ref, v_buf), (r_ref, r_buf)))
    ]
    for copy in copies:
        copy.start()
    for copy in copies:
        copy.wait()
    for i in range(count):
        out_ref[i] = triple(r_buf[i], v_buf[i], ((0,), (0,)))
        for half_ref in rest[:-3]:
            rows = half_ref.shape[1]
            half_ref[i] = out_ref[i, pl.ds(pl.multiple_of(place[6] * rows, rows), rows)]


def list_kernel(chips, held, columns, cols, owner, slot, number, out_ref, words, counts, sems):
    blocks, listed = cols.shape
    span = out_ref.shape[1]
    copies = [
        pltpu.make_async_copy(ref, words.at[i], sems.at[i])
        for i, ref in enumerate((cols, owner, slot))
    ]
    copies += [pltpu.make_async_copy(number, counts, sems.at[3])]
    for copy in copies:
        copy.start()
    for copy in copies:
        copy.wait()
    kinds = lax.broadcasted_iota(I32, (16, listed), 0)
    upto = lax.broadcasted_iota(I32, (listed, listed), 0) <= lanes((listed, listed))
    upto = upto.astype(F32).astype(BF16)
    spots = lax.broadcasted_iota(I32, (chips * span, listed), 0).astype(F32)
    offset = jnp.zeros((16, 1), F32)
    total = jnp.zeros((8, chips * span), F32)
    for i in range(blocks):
        if i == blocks // 2:
            first_half = offset
        col, own, place = words[0, i : i + 1], words[1, i : i + 1], words[2, i : i + 1]
        chip = jnp.where(lanes((1, listed)) < counts[i], own >> 1, chips)
        match = (kinds == chip).astype(F32)
        ranks = jnp.dot(match.astype(BF16), upto, preferred_element_type=F32) + offset
        offset = offset + jnp.sum(match, axis=1, keepdims=True)
        rank = jnp.sum(match * ranks, axis=0, keepdims=True) - 1
        target = jnp.where(chip < chips, chip.astype(F32) * span + rank, -1.0)
        chosen = (spots == target).astype(F32).astype(BF16)
        one = jnp.ones((1, listed), F32)
        fields = jnp.concatenate(
            [
                one,
                ((own & 1) * held + place).astype(F32),
                (col - columns).astype(F32),
                one * i,
                jnp.zeros((4, listed), F32),
            ],
            axis=0,
        )
        total += lax.dot_general(
            fields.astype(BF16), chosen, (((1,), (1,)), ((), ())), preferred_element_type=F32
        )
    row = lax.broadcasted_iota(I32, (8, span), 0)
    for c in range(chips):
        part = total[:, c * span : (c + 1) * span]
        number = jnp.broadcast_to(offset[c : c + 1], (8, span))
        number_half = jnp.broadcast_to(first_half[c : c + 1], (8, span))
        part = jnp.where(row == 4, number_half, part)
        part = jnp.where(row == 0, number, jnp.where(row == 2, part + columns, part))
        out_ref[8 * c : 8 * c + 8] = part


def tile_kernel(core, own_ref, other_ref, out_ref, buf, sems):
    held, _, width = own_ref.shape
    steps, step = buf.shape[:2]
    half = steps // 2
    mine = core[0]
    copies = [
        pltpu.make_async_copy(
            (own_ref if s < half else other_ref).at[pl.ds(s % half * step, step)],
            buf.at[s],
            sems.at[s],
        )
        for s in range(steps)
    ]
    for copy in copies:
        copy.start()
    for s in range(steps):
        copies[s].wait()
        start = (mine if s < half else 1 - mine) * held + s % half * step

        def one(i, _):
            hi, lo = split(buf[s, i])
            out_ref[start + i, :, :width] = hi
            out_ref[start + i, :, width:] = lo
            return 0

        lax.fori_loop(0, step, one, 0, unroll=4)


def gather_kernel(planes, holders, place, own_ref, *refs):
    chips = len(holders)
    pieces, (out_ref, *table_refs) = refs[: -1 - chips], refs[-1 - chips :]
    for holder, table in zip(holders, table_refs):
        base = pieces[holder].shape[0] - 8 * chips
        table[...] = pieces[holder][pl.ds(pl.multiple_of(base + 8 * place[8], 8), 8)].astype(I32)
    count, _, width = own_ref.shape
    quarter = count // 4
    blk = place[1]
    out_ref[planes * count] = jnp.zeros_like(out_ref[planes * count])

    def put(src, start):
        for i in range(src.shape[0]):
            hi, lo = split(src[i])
            out_ref[start + i, :, :width] = hi
            out_ref[start + i, :, width:] = lo

    def put_rows(src, start, half):
        n = out_ref.shape[1] // 2
        rows = pl.ds(pl.multiple_of(half * n, n), n)
        for i in range(quarter):
            hi, lo = split(src[i * n : (i + 1) * n])
            out_ref[start + i, rows, :width] = hi
            out_ref[start + i, rows, width:] = lo

    put(own_ref, blk * count)
    at = 0
    for k in range(1, planes):
        start = lax.rem(blk - k + planes, planes) * count
        if k != planes // 2:
            for p in range(4):
                put(pieces[at + p], start + place[2 + p] * quarter)
            at += 4
            continue
        for p in range(4):
            half = place[6 + p // 2]
            to = start + place[2 + p] * quarter
            put_rows(pieces[at + 2 * p], to, half)
            put_rows(pieces[at + 2 * p + 1], to, 1 - half)
        at += 8


def entry_kernel(second, lists, tiles_ref, proj_ref, out_ref):
    blocks, _, width = out_ref.shape
    zeros = proj_ref.shape[0] - 1
    first, last = (lists[4, 0], lists[0, 0]) if second else (0, lists[4, 0])
    out_ref[...] = jnp.zeros_like(out_ref)

    def multiply(base, n):
        terms = []
        for u in range(n):
            at = base + u
            proj = proj_ref[jnp.where(at < last, lists[2, at], zeros)]
            d = jnp.dot(
                tiles_ref[lists[1, at]],
                jnp.concatenate([proj, proj], axis=0),
                preferred_element_type=F32,
            )
            terms.append(d[:, :width] + d[:, width:])
        for u in range(n):
            block = lists[3, base + u] - (blocks if second else 0)
            out_ref[jnp.clip(block, 0, blocks - 1)] += terms[u]

    def step(s, _):
        multiply(first + s * UNROLL, UNROLL)
        return 0

    number = last - first
    steps = (number + UNROLL // 2 - 1) // UNROLL
    lax.fori_loop(0, steps, step, 0)

    @pl.when(number > steps * UNROLL)
    def _():
        multiply(first + steps * UNROLL, UNROLL // 2)


def final_kernel(second, left_ref, *refs):
    out_ref, buf, sem = refs[-3:]
    sums = refs[1:-3] if second else refs[:-3]
    blocks = buf.shape[0]
    start = blocks if second else 0
    for i in range(blocks):
        total = functools.reduce(jnp.add, [r[i] for r in sums])
        buf[i] = triple(left_ref[start + i], total, ((1,), (0,)))
    copy = pltpu.make_async_copy(buf, out_ref.at[pl.ds(start, blocks)], sem)
    copy.start()
    copy.wait()


def call(kernel, prefetch, ins, out, scratch, args, estimate, limit, grid=(), out_spec=VMEM, aliases={}):
    return pl.pallas_call(
        kernel,
        out_shape=out,
        grid_spec=pltpu.PrefetchScalarGridSpec(
            num_scalar_prefetch=prefetch,
            grid=grid,
            in_specs=ins,
            out_specs=out_spec,
            scratch_shapes=scratch,
        ),
        compiler_params=pltpu.CompilerParams(vmem_limit_bytes=limit),
        cost_estimate=estimate,
        input_output_aliases=aliases,
    )(*args)


def work(
    vectors, left, right, tiles, pair_cols, pair_owner, pair_slot, pair_counts
):
    rows, planes = lax.axis_size("rows"), lax.axis_size("blk")
    row, blk = lax.axis_index("rows"), lax.axis_index("blk")
    blocks, fine, coarse = left.shape
    vecs = vectors.shape[1]
    count = right.shape[0]
    held = tiles.shape[0]
    listed = pair_cols.shape[1]
    chips = rows // 2
    cap = blocks * listed // chips
    quarter = count // 4
    core, chip = row & 1, row >> 1
    b0, b1 = chip & 1, (chip >> 1) & 1

    def physical(mask, core_at):
        return mask if core_at == 0 else (mask & ~3) | ((mask & 1) << 1) | ((mask >> 1) & 1)

    def across(mask):
        return [(r, r ^ (physical(mask, r % 2) << 1)) for r in range(rows)]

    def swap(x):
        return lax.ppermute(x, "rows", [(r, r ^ 1) for r in range(rows)])

    def turn(x, k):
        return lax.ppermute(x, "blk", [(b, (b + k) % planes) for b in range(planes)])

    mine = jnp.where(core == 0, b0, 2 + b1)
    theirs = jnp.where(core == 0, 2 + b1, b0)
    row_half = jnp.where(core == 0, b1, b0)
    their_half = jnp.where(core == 0, b0, b1)
    place = jnp.stack([mine, blk, mine, mine ^ 1, theirs, theirs ^ 1, row_half, their_half, chip]).astype(I32)

    v = vectors.reshape(count, fine, vecs)
    v, right = in_hbm(v), in_hbm(right)

    def project(n, out):
        return call(
            project_kernel, 1, [HBM, HBM], out,
            [pltpu.VMEM((n, fine, vecs), F32)] * 2 + [pltpu.SemaphoreType.DMA((2,))],
            (place, v, right), cost(2 * n * 128**3 * 3, 2 * n * 65536), 8 * MIB,
            out_spec=[VMEM] * len(out) if isinstance(out, list) else VMEM,
        )

    middle = planes // 2
    sent, sent_half = project(
        quarter,
        [
            jax.ShapeDtypeStruct((quarter, coarse, vecs), F32),
            jax.ShapeDtypeStruct((quarter, coarse // 2, vecs), F32),
        ],
    )
    arrived = {k: turn(sent_half if k == middle else sent, k) for k in range(1, planes)}
    other_tiles = swap(tiles)

    span = pl.cdiv(cap, 128) * 128
    lists = call(
        functools.partial(list_kernel, chips, held, planes * count), 0, [HBM] * 4,
        jax.ShapeDtypeStruct((chips * 8, span), F32),
        [
            pltpu.VMEM((3, blocks, listed), I32),
            pltpu.SMEM((blocks,), I32),
            pltpu.SemaphoreType.DMA((4,)),
        ],
        (in_hbm(pair_cols), in_hbm(pair_owner), in_hbm(pair_slot), in_hbm(pair_counts)),
        cost(10**8, 16384), 8 * MIB,
    )
    own = project(count, jax.ShapeDtypeStruct((count, coarse, vecs), F32))
    packed = call(
        tile_kernel, 1, [HBM, pl.BlockSpec(memory_space=pl.ANY)],
        jax.ShapeDtypeStruct((2 * held, coarse, 2 * coarse), BF16),
        [pltpu.VMEM((held // 4, 8, coarse, coarse), F32), pltpu.SemaphoreType.DMA((held // 4,))],
        (core.reshape(1).astype(I32), in_hbm(tiles), other_tiles),
        cost(held * 65536 * 4, held * 65536 * 4), 2 * held * 65536 + 4 * MIB,
    )

    def spread(x, mask=1):
        return lax.ppermute(x, "rows", across(mask))

    pieces = []
    for k in range(1, planes):
        z = arrived[k]
        if k == middle:
            z = jnp.concatenate([z.reshape(-1, vecs), lists], axis=0)
            rest = spread(z, 2)
            x, x_rest = spread(z), spread(rest)
            ridden = {1: x, 2: rest, 3: x_rest}
            pieces += [z, rest, x, x_rest, swap(z), swap(rest)]
            pieces += [swap(x), swap(x_rest)]
        else:
            x = spread(z)
            pieces += [z, x, swap(z), swap(x)]

    holders = [len(pieces)] + [next(i for i, p in enumerate(pieces) if p is ridden[m]) for m in (1, 2, 3)]
    pieces += [lists]
    from_chip = [lists] + [ridden[m][-8 * chips :] for m in (1, 2, 3)]
    for bit in (1 << j for j in range(2, chips.bit_length() - 1)):
        for m in range(bit):
            from_chip.append(lax.ppermute(from_chip[m], "rows", across(bit)))
            holders.append(len(pieces))
            pieces.append(from_chip[-1])
    proj, *tables = call(
        functools.partial(gather_kernel, planes, holders), 1, [VMEM] * (1 + len(pieces)),
        [jax.ShapeDtypeStruct((planes * count + 1, coarse, 2 * vecs), BF16)]
        + [jax.ShapeDtypeStruct((8, span), I32)] * chips,
        [], (place, own, *pieces), cost(10**6, 3 * planes * count * 32768), 16 * MIB,
        out_spec=[VMEM] * (1 + chips),
    )

    total = {
        (m, h): [
            call(
                functools.partial(entry_kernel, h), 1, [VMEM, VMEM],
                jax.ShapeDtypeStruct((blocks // 2, coarse, vecs), F32),
                [], (tables[m], packed, proj),
                cost(cap * 128**3 * 4, 4 * MIB), 12 * MIB,
            )
        ]
        for m in range(chips)
        for h in range(2)
    }
    for m in masks_of(chips):
        bit = m & -m
        for h in range(2):
            value = functools.reduce(jnp.add, total[m, h])
            total[m ^ bit, h].append(lax.ppermute(value, "rows", across(bit)))
    result = []
    for h in range(2):
        result = [
            call(
                functools.partial(final_kernel, h), 0,
                [VMEM] + [HBM] * len(result) + [VMEM] * len(total[0, h]),
                jax.ShapeDtypeStruct((blocks, fine, vecs), F32),
                [pltpu.VMEM((blocks // 2, fine, vecs), F32), pltpu.SemaphoreType.DMA(())],
                (left, *result, *total[0, h]), cost(blocks * 128**3 * 3, MIB), 8 * MIB,
                out_spec=HBM, aliases={1: 0} if result else {},
            )
        ]
    return result[0].reshape(blocks * fine, vecs)


def masks_of(chips):
    return sorted(range(1, chips), key=lambda m: (m & -m, -m))


def solution(mesh):
    return jax.shard_map(
        work,
        mesh=mesh,
        in_specs=(
            P("blk", None),
            P(("rows", "blk"), None, None),
            P("blk", None, None),
            P("rows", None, None),
            P(("rows", "blk"), None),
            P(("rows", "blk"), None),
            P(("rows", "blk"), None),
            P(("rows", "blk")),
        ),
        out_specs=P(("rows", "blk"), None),
        check_vma=False,
    )
```

```python
import functools

import jax
import jax.numpy as jnp
from jax import lax
from jax.experimental import pallas as pl
from jax.experimental.pallas import tpu as pltpu
from jax.sharding import PartitionSpec as P


F32 = jnp.float32
BF16 = jnp.bfloat16
I32 = jnp.int32
UNROLL = 16
MIB = 1 << 20


VMEM = pl.BlockSpec(memory_space=pltpu.VMEM)
HBM = pl.BlockSpec(memory_space=pltpu.HBM)


def in_hbm(x):
    return pltpu.with_memory_space_constraint(x, pltpu.HBM)


def cost(flops, nbytes):
    return pl.CostEstimate(flops=flops, bytes_accessed=nbytes, transcendentals=0)


def split(x):
    hi = x.astype(BF16)
    return hi, (x - hi.astype(F32)).astype(BF16)


def lanes(shape):
    return lax.broadcasted_iota(I32, shape, len(shape) - 1)


def triple(a, b, dims):
    a_hi, a_lo = split(a)
    b_hi, b_lo = split(b)

    def dot(x, y):
        return lax.dot_general(x, y, (dims, ((), ())), preferred_element_type=F32)

    return dot(a_hi, b_hi) + dot(a_hi, b_lo) + dot(a_lo, b_hi)


def project_kernel(place, v_ref, r_ref, out_ref, *rest):
    v_buf, r_buf, sems = rest[-3:]
    count = v_buf.shape[0]
    first = place[0] * count if count < v_ref.shape[0] else 0
    copies = [
        pltpu.make_async_copy(ref.at[pl.ds(first, count)], buf, sems.at[i])
        for i, (ref, buf) in enumerate(((v_ref, v_buf), (r_ref, r_buf)))
    ]
    for copy in copies:
        copy.start()
    for copy in copies:
        copy.wait()
    for i in range(count):
        out_ref[i] = triple(r_buf[i], v_buf[i], ((0,), (0,)))
        for half_ref in rest[:-3]:
            rows = half_ref.shape[1]
            half_ref[i] = out_ref[i, pl.ds(pl.multiple_of(place[6] * rows, rows), rows)]


def list_kernel(chips, held, columns, cols, owner, slot, number, out_ref, words, counts, sems):
    blocks, listed = cols.shape
    span = out_ref.shape[1]
    copies = [
        pltpu.make_async_copy(ref, words.at[i], sems.at[i])
        for i, ref in enumerate((cols, owner, slot))
    ]
    copies += [pltpu.make_async_copy(number, counts, sems.at[3])]
    for copy in copies:
        copy.start()
    for copy in copies:
        copy.wait()
    kinds = lax.broadcasted_iota(I32, (16, listed), 0)
    upto = lax.broadcasted_iota(I32, (listed, listed), 0) <= lanes((listed, listed))
    upto = upto.astype(F32).astype(BF16)
    spots = lax.broadcasted_iota(I32, (chips * span, listed), 0).astype(F32)
    offset = jnp.zeros((16, 1), F32)
    total = jnp.zeros((8, chips * span), F32)
    for i in range(blocks):
        if i == blocks // 2:
            first_half = offset
        col, own, place = words[0, i : i + 1], words[1, i : i + 1], words[2, i : i + 1]
        chip = jnp.where(lanes((1, listed)) < counts[i], own >> 1, chips)
        match = (kinds == chip).astype(F32)
        ranks = jnp.dot(match.astype(BF16), upto, preferred_element_type=F32) + offset
        offset = offset + jnp.sum(match, axis=1, keepdims=True)
        rank = jnp.sum(match * ranks, axis=0, keepdims=True) - 1
        target = jnp.where(chip < chips, chip.astype(F32) * span + rank, -1.0)
        chosen = (spots == target).astype(F32).astype(BF16)
        one = jnp.ones((1, listed), F32)
        fields = jnp.concatenate(
            [
                one,
                ((own & 1) * held + place).astype(F32),
                (col - columns).astype(F32),
                one * i,
                jnp.zeros((4, listed), F32),
            ],
            axis=0,
        )
        total += lax.dot_general(
            fields.astype(BF16), chosen, (((1,), (1,)), ((), ())), preferred_element_type=F32
        )
    row = lax.broadcasted_iota(I32, (8, span), 0)
    for c in range(chips):
        part = total[:, c * span : (c + 1) * span]
        number = jnp.broadcast_to(offset[c : c + 1], (8, span))
        number_half = jnp.broadcast_to(first_half[c : c + 1], (8, span))
        part = jnp.where(row == 4, number_half, part)
        part = jnp.where(row == 0, number, jnp.where(row == 2, part + columns, part))
        out_ref[8 * c : 8 * c + 8] = part


def tile_kernel(core, own_ref, other_ref, out_ref, buf, sems):
    held, _, width = own_ref.shape
    steps, step = buf.shape[:2]
    half = steps // 2
    mine = core[0]
    copies = [
        pltpu.make_async_copy(
            (own_ref if s < half else other_ref).at[pl.ds(s % half * step, step)],
            buf.at[s],
            sems.at[s],
        )
        for s in range(steps)
    ]
    for copy in copies:
        copy.start()
    for s in range(steps):
        copies[s].wait()
        start = (mine if s < half else 1 - mine) * held + s % half * step

        def one(i, _):
            hi, lo = split(buf[s, i])
            out_ref[start + i, :, :width] = hi
            out_ref[start + i, :, width:] = lo
            return 0

        lax.fori_loop(0, step, one, 0, unroll=4)


def gather_kernel(planes, holders, place, own_ref, *refs):
    chips = len(holders)
    pieces, (out_ref, *table_refs) = refs[: -1 - chips], refs[-1 - chips :]
    for holder, table in zip(holders, table_refs):
        base = pieces[holder].shape[0] - 8 * chips
        table[...] = pieces[holder][pl.ds(pl.multiple_of(base + 8 * place[8], 8), 8)].astype(I32)
    count, _, width = own_ref.shape
    quarter = count // 4
    blk = place[1]
    out_ref[planes * count] = jnp.zeros_like(out_ref[planes * count])

    def put(src, start):
        for i in range(src.shape[0]):
            hi, lo = split(src[i])
            out_ref[start + i, :, :width] = hi
            out_ref[start + i, :, width:] = lo

    def put_rows(src, start, half):
        n = out_ref.shape[1] // 2
        rows = pl.ds(pl.multiple_of(half * n, n), n)
        for i in range(quarter):
            hi, lo = split(src[i * n : (i + 1) * n])
            out_ref[start + i, rows, :width] = hi
            out_ref[start + i, rows, width:] = lo

    put(own_ref, blk * count)
    at = 0
    for k in range(1, planes):
        start = lax.rem(blk - k + planes, planes) * count
        if k != planes // 2:
            for p in range(4):
                put(pieces[at + p], start + place[2 + p] * quarter)
            at += 4
            continue
        for p in range(4):
            half = place[6 + p // 2]
            to = start + place[2 + p] * quarter
            put_rows(pieces[at + 2 * p], to, half)
            put_rows(pieces[at + 2 * p + 1], to, 1 - half)
        at += 8


def entry_kernel(half, lists, tiles_ref, proj_ref, out_ref):
    blocks, _, width = out_ref.shape
    zeros = proj_ref.shape[0] - 1
    first = lists[4, 0] if half == 1 else 0
    last = lists[4, 0] if half == 0 else lists[0, 0]
    out_ref[...] = jnp.zeros_like(out_ref)

    def multiply(base, n):
        terms = []
        for u in range(n):
            at = base + u
            proj = proj_ref[jnp.where(at < last, lists[2, at], zeros)]
            d = jnp.dot(
                tiles_ref[lists[1, at]],
                jnp.concatenate([proj, proj], axis=0),
                preferred_element_type=F32,
            )
            terms.append(d[:, :width] + d[:, width:])
        for u in range(n):
            block = lists[3, base + u] - (blocks if half == 1 else 0)
            out_ref[jnp.clip(block, 0, blocks - 1)] += terms[u]

    def step(s, _):
        multiply(first + s * UNROLL, UNROLL)
        return 0

    number = last - first
    steps = (number + UNROLL // 2 - 1) // UNROLL
    lax.fori_loop(0, steps, step, 0)

    @pl.when(number > steps * UNROLL)
    def _():
        multiply(first + steps * UNROLL, UNROLL // 2)


def final_kernel(left_ref, *refs):
    sums, out_ref = refs[:-1], refs[-1]
    for i in range(out_ref.shape[0]):
        total = functools.reduce(jnp.add, [r[i] for r in sums])
        out_ref[i] = triple(left_ref[i], total, ((1,), (0,)))


def call(kernel, prefetch, ins, out, scratch, args, estimate, limit, grid=(), out_spec=VMEM):
    return pl.pallas_call(
        kernel,
        out_shape=out,
        grid_spec=pltpu.PrefetchScalarGridSpec(
            num_scalar_prefetch=prefetch,
            grid=grid,
            in_specs=ins,
            out_specs=out_spec,
            scratch_shapes=scratch,
        ),
        compiler_params=pltpu.CompilerParams(vmem_limit_bytes=limit),
        cost_estimate=estimate,
    )(*args)


def work(
    vectors, left, right, tiles, pair_cols, pair_owner, pair_slot, pair_counts
):
    rows, planes = lax.axis_size("rows"), lax.axis_size("blk")
    row, blk = lax.axis_index("rows"), lax.axis_index("blk")
    blocks, fine, coarse = left.shape
    vecs = vectors.shape[1]
    count = right.shape[0]
    held = tiles.shape[0]
    listed = pair_cols.shape[1]
    chips = rows // 2
    cap = blocks * listed // chips
    quarter = count // 4
    core, chip = row & 1, row >> 1
    b0, b1 = chip & 1, (chip >> 1) & 1

    def physical(mask, core_at):
        return mask if core_at == 0 else (mask & ~3) | ((mask & 1) << 1) | ((mask >> 1) & 1)

    def across(mask):
        return [(r, r ^ (physical(mask, r % 2) << 1)) for r in range(rows)]

    def swap(x):
        return lax.ppermute(x, "rows", [(r, r ^ 1) for r in range(rows)])

    def turn(x, k):
        return lax.ppermute(x, "blk", [(b, (b + k) % planes) for b in range(planes)])

    mine = jnp.where(core == 0, b0, 2 + b1)
    theirs = jnp.where(core == 0, 2 + b1, b0)
    row_half = jnp.where(core == 0, b1, b0)
    their_half = jnp.where(core == 0, b0, b1)
    place = jnp.stack([mine, blk, mine, mine ^ 1, theirs, theirs ^ 1, row_half, their_half, chip]).astype(I32)

    v = vectors.reshape(count, fine, vecs)
    v, right = in_hbm(v), in_hbm(right)

    def project(n, out):
        return call(
            project_kernel, 1, [HBM, HBM], out,
            [pltpu.VMEM((n, fine, vecs), F32)] * 2 + [pltpu.SemaphoreType.DMA((2,))],
            (place, v, right), cost(2 * n * 128**3 * 3, 2 * n * 65536), 8 * MIB,
            out_spec=[VMEM] * len(out) if isinstance(out, list) else VMEM,
        )

    middle = planes // 2
    sent, sent_half = project(
        quarter,
        [
            jax.ShapeDtypeStruct((quarter, coarse, vecs), F32),
            jax.ShapeDtypeStruct((quarter, coarse // 2, vecs), F32),
        ],
    )
    arrived = {k: turn(sent_half if k == middle else sent, k) for k in range(1, planes)}
    other_tiles = swap(tiles)

    span = pl.cdiv(cap, 128) * 128
    lists = call(
        functools.partial(list_kernel, chips, held, planes * count), 0, [HBM] * 4,
        jax.ShapeDtypeStruct((chips * 8, span), F32),
        [
            pltpu.VMEM((3, blocks, listed), I32),
            pltpu.SMEM((blocks,), I32),
            pltpu.SemaphoreType.DMA((4,)),
        ],
        (in_hbm(pair_cols), in_hbm(pair_owner), in_hbm(pair_slot), in_hbm(pair_counts)),
        cost(10**8, 16384), 8 * MIB,
    )
    own = project(count, jax.ShapeDtypeStruct((count, coarse, vecs), F32))
    packed = call(
        tile_kernel, 1, [HBM, pl.BlockSpec(memory_space=pl.ANY)],
        jax.ShapeDtypeStruct((2 * held, coarse, 2 * coarse), BF16),
        [pltpu.VMEM((held // 4, 8, coarse, coarse), F32), pltpu.SemaphoreType.DMA((held // 4,))],
        (core.reshape(1).astype(I32), in_hbm(tiles), other_tiles),
        cost(held * 65536 * 4, held * 65536 * 4), 2 * held * 65536 + 4 * MIB,
    )

    def spread(x, mask=1):
        return lax.ppermute(x, "rows", across(mask))

    pieces = []
    for k in range(1, planes):
        z = arrived[k]
        if k == middle:
            z = jnp.concatenate([z.reshape(-1, vecs), lists], axis=0)
            rest = spread(z, 2)
            x, x_rest = spread(z), spread(rest)
            ridden = {1: x, 2: rest, 3: x_rest}
            pieces += [z, rest, x, x_rest, swap(z), swap(rest)]
            pieces += [swap(x), swap(x_rest)]
        else:
            x = spread(z)
            pieces += [z, x, swap(z), swap(x)]

    holders = [len(pieces)] + [next(i for i, p in enumerate(pieces) if p is ridden[m]) for m in (1, 2, 3)]
    pieces += [lists]
    from_chip = [lists] + [ridden[m][-8 * chips :] for m in (1, 2, 3)]
    for bit in (1 << j for j in range(2, chips.bit_length() - 1)):
        for m in range(bit):
            from_chip.append(lax.ppermute(from_chip[m], "rows", across(bit)))
            holders.append(len(pieces))
            pieces.append(from_chip[-1])
    proj, *tables = call(
        functools.partial(gather_kernel, planes, holders), 1, [VMEM] * (1 + len(pieces)),
        [jax.ShapeDtypeStruct((planes * count + 1, coarse, 2 * vecs), BF16)]
        + [jax.ShapeDtypeStruct((8, span), I32)] * chips,
        [], (place, own, *pieces), cost(10**6, 3 * planes * count * 32768), 16 * MIB,
        out_spec=[VMEM] * (1 + chips),
    )

    def sum_of(m, half=None):
        return call(
            functools.partial(entry_kernel, half), 1, [VMEM, VMEM],
            jax.ShapeDtypeStruct((blocks if half is None else blocks // 2, coarse, vecs), F32),
            [], (tables[m], packed, proj), cost(cap * 128**3 * 4, 4 * MIB), 12 * MIB,
        )

    masks = masks_of(chips)
    total = {m: [sum_of(m)] for m in range(chips) if m != masks[0]}
    arriving = []
    for half in range(2):
        value = sum_of(masks[0], half)
        arriving.append(lax.ppermute(value, "rows", across(1)))
    total[masks[0] ^ 1].append(jnp.concatenate(arriving, axis=0))
    for m in masks[1:]:
        bit = m & -m
        value = functools.reduce(jnp.add, total[m])
        total[m ^ bit].append(lax.ppermute(value, "rows", across(bit)))
    result = call(
        final_kernel, 0, [VMEM] * (1 + len(total[0])),
        jax.ShapeDtypeStruct((blocks, fine, vecs), F32),
        [], (left, *total[0]), cost(2 * blocks * 128**3 * 3, 2 * MIB), 8 * MIB,
    )
    return result.reshape(blocks * fine, vecs)


def masks_of(chips):
    return sorted(range(1, chips), key=lambda m: (m & -m, -m))


def solution(mesh):
    return jax.shard_map(
        work,
        mesh=mesh,
        in_specs=(
            P("blk", None),
            P(("rows", "blk"), None, None),
            P("blk", None, None),
            P("rows", None, None),
            P(("rows", "blk"), None),
            P(("rows", "blk"), None),
            P(("rows", "blk"), None),
            P(("rows", "blk")),
        ),
        out_specs=P(("rows", "blk"), None),
        check_vma=False,
    )
```
